256 devices in a mesh: tm: 4 (over z_lo), elem: 64 (over z_hi, x, y, core).
Axes of the slice: x: 4, y: 4, z: 8 (z_hi: 2, z_lo: 4; z = z_hi * 4 + z_lo), core: 2. Of those that a mesh axis runs over, the one named last changes fastest.
Arguments:
- state: float32 [16, 5, 64, 125, 128], P('tm', None, 'elem'), may hold values from -6 to 6
- metric_scale: float32 [64, 125, 128], P('elem'), may hold values from 0.1 to 0.4
- flux_jacobians: float32 [3, 5, 5], replicated, may hold values from -1.5 to 1.5, as said below
- preconditioner: float32 [16, 5, 5, 64, 128], P('tm', None, None, 'elem'), may hold values from -0.04 to 0.24
- inflow: float32 [16, 5, 64, 25], P('tm', None, 'elem'), may hold values from -6 to 6
Outputs:
- new_state: float32 [16, 5, 64, 125, 128], P('tm', None, 'elem')
- final_residual: float32 [16, 5, 64, 125, 128], P('tm', None, 'elem')
The draws below stay inside these ranges and needn't reach their ends.
Inputs may be any that keep to these rules, and one draw needn't show every extreme that they name: `flux_jacobians`: symmetric in its last two dimensions.
All inputs are finite; a program needn't handle non-finite values.
Results may differ from the reference program's by a relative error of at most 0.0001.
Values sent between devices are 32-bit elements; how exact they have to be, the bound alone decides.
A program may use at most 128 MiB of HBM per device.

```python
import math
import jax
import jax.numpy as jnp
import numpy as np
from jax import lax

NI = 16
NV = 5
PR = 8
PASSES = 3
NAX = 128
COLS = 64
NCIRC = 8


def draw_flux_jacobians(key, part):
    sampled = jnp.clip(jax.random.normal(key, (3, NV, NV), jnp.float32) * 0.45, -1.5, 1.5)
    return 0.5 * (sampled + jnp.swapaxes(sampled, 1, 2))


def draw_preconditioner(key, part):
    key_scale = jax.random.fold_in(key, 11)
    key_mix = jax.random.fold_in(key, 23)
    scales = jnp.exp(jax.random.uniform(key_scale, (NI, 1, 1, COLS, NAX), jnp.float32, math.log(0.05), math.log(0.2)))
    mixing = jax.random.uniform(key_mix, (NI, NV, NV, COLS, NAX), jnp.float32, -0.2, 0.2)
    identity = jnp.eye(NV, dtype=jnp.float32)[None, :, :, None, None]
    return scales * (identity * (1.0 + mixing) + (1.0 - identity) * mixing)


def shard_levels(rng, shape, cuts, least, top_value):
    factor_of, own = 1.0, jax.random.fold_in(rng, 6)
    for dim, parts in cuts:
        draws = jnp.exp(jax.random.uniform(jax.random.fold_in(own, dim), (parts,), jnp.float32, least / len(cuts), top_value / len(cuts)))
        factor_of = factor_of * jnp.repeat(draws, shape[dim] // parts).reshape([-1 if axis == dim else 1 for axis in range(len(shape))])
    return factor_of


def bell_draw(key, extent, spread, bound, cuts=(), held_as=jnp.bfloat16):
    values = jax.random.normal(key, extent, jnp.float32) * spread
    if len(cuts) > 0:
        values = shard_levels(key, extent, cuts, -0.22, 0.18) * values
    return jnp.clip(values, min=-bound, max=bound).astype(held_as)


def setup_inputs(seed: int = 0) -> dict:
    key_of = jax.random.split(jax.random.key(seed), 6)
    return {
        "state": bell_draw(key_of[0], (NI, NV, COLS, 125, NAX), 1.0, 6.0, ((0, 4), (2, 64)), jnp.float32),
        "metric_scale": jnp.clip(jnp.exp(math.log(0.4) - 1.3862944 * jax.random.uniform(key_of[1], (COLS, 125, NAX), jnp.float32) ** shard_levels(key_of[1], (COLS, 125, NAX), ((0, 64),), -0.2, 0.2)), 0.1, 0.4),
        "flux_jacobians": draw_flux_jacobians(jax.random.fold_in(key_of[5], 71), 0),
        "preconditioner": draw_preconditioner(jax.random.fold_in(key_of[5], 71), 0),
        "inflow": bell_draw(key_of[4], (NI, NV, COLS, 25), 1.0, 6.0, ((0, 4), (2, 64)), jnp.float32),
    }


precise = lax.Precision.HIGHEST

def gll_derivative():
    points = np.array([-1.0, -math.sqrt(3.0 / 7.0), 0.0, math.sqrt(3.0 / 7.0), 1.0])
    legendre = (35.0 * points ** 4 - 30.0 * points ** 2 + 3.0) / 8.0
    identity = np.eye(5, dtype=bool)
    spacing = np.where(identity, 1.0, points[:, None] - points[None, :])
    matrix = legendre[:, None] / legendre[None, :] / spacing
    corner = np.array([-5.0, 0.0, 0.0, 0.0, 5.0])[None, :]
    return np.where(identity, corner, matrix)

def spectral_rows(row_ids, col_ids, count):
    offset = row_ids[:, None] - col_ids[None, :]
    parity = 1.0 - 2.0 * jnp.remainder(offset, 2).astype(jnp.float32)
    angle = jnp.pi * offset.astype(jnp.float32) / count
    diagonal = offset == 0
    sine = jnp.where(diagonal, 1.0, jnp.sin(angle))
    return jnp.where(diagonal, 0.0, 0.5 * parity * jnp.cos(angle) / sine)

def apply_matrix(matrix, values):
    return jnp.einsum('vw,nw...->nv...', matrix, values, precision=precise)

def lift_faces(lows, highs, beyond_low, beyond_high, matrix, damping, node_axis):
    jump_high = beyond_high - highs
    jump_low = beyond_low - lows
    high_term = 0.5 * (apply_matrix(matrix, jump_high) - damping * jump_high)
    low_term = -0.5 * (apply_matrix(matrix, jump_low) + damping * jump_low)
    middle = jnp.zeros_like(lows)
    return jnp.stack([low_term, middle, middle, middle, high_term], axis=node_axis)

def reference(state, metric_scale, flux_jacobians, preconditioner, inflow):
    derivative = jnp.asarray(gll_derivative(), dtype=jnp.float32)
    damping = lax.optimization_barrier(jnp.max(lax.optimization_barrier(jnp.sum(jnp.abs(flux_jacobians), axis=2)), axis=1))
    instances = jnp.arange(NI, dtype=jnp.int32)
    coupling = spectral_rows(instances, instances, NI)
    spectral = jnp.dot(coupling, state.reshape(NI, -1), precision=precise, preferred_element_type=jnp.float32).reshape(state.shape)
    half_col = PR // 2
    grid_shape = (NI, NV, NCIRC, PR, 5, 5, 5, NAX)
    metric = jnp.roll(metric_scale, half_col, axis=0).reshape((1, 1) + grid_shape[2:])
    inflow_nodes = jnp.roll(inflow, half_col, axis=2).reshape(NI, NV, NCIRC, PR, 5, 5, 1)
    reflect = jnp.array([1.0, 1.0, -1.0, 1.0, 1.0], dtype=jnp.float32).reshape(1, NV, 1, 1, 1, 1, 1)
    outputs = ('nvcrpjka', 'nvcripka', 'nvcrijpa')
    inputs = ('pi,nvcrijka', 'pj,nvcrijka', 'pk,nvcrijka')

    def full_residual(current):
        fields = jnp.roll(current, half_col, axis=2).reshape(grid_shape)
        volume = jnp.zeros_like(fields)
        for direction in range(3):
            fluxes = apply_matrix(flux_jacobians[direction], fields)
            volume = volume + jnp.einsum(inputs[direction] + '->' + outputs[direction], derivative, fluxes, precision=precise)
        lows = fields[:, :, :, :, 0]
        highs = fields[:, :, :, :, 4]
        surface = lift_faces(lows, highs, jnp.roll(highs, 1, axis=2), jnp.roll(lows, -1, axis=2), flux_jacobians[0], damping[0], 4)
        lows = fields[:, :, :, :, :, 0]
        highs = fields[:, :, :, :, :, 4]
        beyond_high = jnp.concatenate([lows[:, :, :, 1:], reflect * highs[:, :, :, -1:]], axis=3)
        beyond_low = jnp.concatenate([reflect * lows[:, :, :, :1], highs[:, :, :, :-1]], axis=3)
        surface = surface + lift_faces(lows, highs, beyond_low, beyond_high, flux_jacobians[1], damping[1], 5)
        lows = fields[:, :, :, :, :, :, 0]
        highs = fields[:, :, :, :, :, :, 4]
        beyond_high = jnp.concatenate([lows[..., 1:], highs[..., -1:]], axis=6)
        beyond_low = jnp.concatenate([inflow_nodes, highs[..., :-1]], axis=6)
        surface = surface + lift_faces(lows, highs, beyond_low, beyond_high, flux_jacobians[2], damping[2], 6)
        spatial = (metric * (volume + 10.0 * surface)).reshape(state.shape)
        return jnp.roll(spatial, -half_col, axis=2) + spectral
    iterate = state
    for sweep_index in range(PASSES):
        update = jnp.einsum('nvwca,nwcqa->nvcqa', preconditioner, full_residual(iterate), precision=precise)
        iterate = iterate - update
    return (iterate, full_residual(iterate))
```

```python
import functools
import math

import jax
import jax.numpy as jnp
import numpy as np
from jax import lax
from jax.experimental import pallas as pl
from jax.experimental.pallas import tpu as pltpu
from jax.sharding import PartitionSpec as P

NI = 16
NV = 5
PR = 8
PASSES = 3
ROWS = 128
NODES = 125
FACE = 25
CHUNK = 32
MESH = pl.DeviceIdType.MESH
F32 = jnp.float32
BF16 = jnp.bfloat16


def gll_derivative():
    points = np.array([-1.0, -math.sqrt(3.0 / 7.0), 0.0, math.sqrt(3.0 / 7.0), 1.0])
    legendre = (35.0 * points**4 - 30.0 * points**2 + 3.0) / 8.0
    identity = np.eye(5, dtype=bool)
    spacing = np.where(identity, 1.0, points[:, None] - points[None, :])
    matrix = legendre[:, None] / legendre[None, :] / spacing
    corner = np.array([-5.0, 0.0, 0.0, 0.0, 5.0])[None, :]
    return np.where(identity, corner, matrix)


def coupling(offset):
    if offset % NI == 0:
        return 0.0
    angle = math.pi * offset / NI
    return 0.5 * (1.0 - 2.0 * (offset % 2)) * math.cos(angle) / math.sin(angle)


def patterns():
    table = gll_derivative()
    node = np.arange(NODES)
    index = [node // 25, (node // 5) % 5, node % 5]
    out = np.zeros((12, ROWS, ROWS))
    for d in range(3):
        others = [index[o] for o in range(3) if o != d]
        same = np.ones((NODES, NODES), bool)
        for o in others:
            same &= o[:, None] == o[None, :]
        out[d, :NODES, :NODES] = np.where(same, table[index[d][:, None], index[d][None, :]], 0.0)
        high, low = index[d] == 4, index[d] == 0
        out[d, node, node] += np.where(high, -5.0, 0.0) + np.where(low, 5.0, 0.0)
        out[3 + d, node, node] = np.where(high | low, 5.0, 0.0)
        for side, face in enumerate((high, low)):
            dest = node[face]
            for v in range(NV):
                out[6 + 2 * d + side, dest, FACE * v + np.arange(FACE)] = 5.0
    return out.astype(np.float32)


def split(value):
    high = value.astype(BF16)
    low = (value - high.astype(F32)).astype(BF16)
    return high, low


def kernel(
    state_ref, metric_ref, jac_ref, pre_ref, inflow_ref, pat_ref, new_ref, res_ref,
    us, u, spec, metric, inflow_cols, k_loc, k_tr, x_hi, x_lo, t_hi, t_lo, r, ax,
    stage, faces, raw, cross_out, cross_in, edge_out, edge_in,
    face_s, face_r, raw_s, raw_r, cross_s, cross_r, edge_s, edge_r,
):
    t = lax.axis_index("tm")
    e = lax.axis_index("elem")
    inner = jnp.logical_or(t == 1, t == 2)
    outer = jnp.logical_not(inner)
    ahead = t < 2
    beside = jnp.where(inner, jnp.where(t == 1, 0, 3), jnp.where(t == 0, 1, 2))
    opposite = jnp.where(inner, 3 - t, t)
    at_top = lax.rem(e, PR) == PR // 2 - 1
    at_bottom = lax.rem(e, PR) == PR // 2
    following = lax.rem(e + PR, 64)
    preceding = lax.rem(e + 64 - PR, 64)
    above = lax.rem(e + 1, 64)
    below = lax.rem(e + 63, 64)

    barrier = pltpu.get_barrier_semaphore()
    for peer in (following, preceding, above, below):
        pl.semaphore_signal(barrier, inc=1, device_id=(t, peer), device_id_type=MESH)
    for step in (1, 3):
        pl.semaphore_signal(barrier, inc=1, device_id=(lax.rem(t + step, 4), e), device_id_type=MESH)

    def face_copy(x, p, f):
        peer = (preceding, following, below, above)[f]
        return pltpu.make_async_remote_copy(
            src_ref=stage.at[x, p, f], dst_ref=faces.at[x, p, f],
            send_sem=face_s.at[x, p, f], recv_sem=face_r.at[x, p, f],
            device_id=(t, peer), device_id_type=MESH,
        )

    def raw_copy(v):
        return pltpu.make_async_remote_copy(
            src_ref=us.at[v], dst_ref=raw.at[v], send_sem=raw_s.at[v], recv_sem=raw_r.at[v],
            device_id=(beside, e), device_id_type=MESH,
        )

    def cross_copy(p, v):
        return pltpu.make_async_remote_copy(
            src_ref=cross_out.at[p, v], dst_ref=cross_in.at[p, v],
            send_sem=cross_s.at[p, v], recv_sem=cross_r.at[p, v],
            device_id=(opposite, e), device_id_type=MESH,
        )

    def edge_copy(p, v):
        return pltpu.make_async_remote_copy(
            src_ref=edge_out.at[p, v], dst_ref=edge_in.at[p, v],
            send_sem=edge_s.at[p, v], recv_sem=edge_r.at[p, v],
            device_id=(beside, e), device_id_type=MESH,
        )

    tail = pl.ds(ROWS - 8, 8)
    metric[tail, :] = jnp.zeros((8, 128), F32)
    metric[pl.ds(0, NODES), :] = metric_ref[...]
    for v in range(NV):
        for n in range(4):
            us[v, n, tail, :] = jnp.zeros((8, 128), F32)
            us[v, n, pl.ds(0, NODES), :] = state_ref[n, v]
    ax[:, tail, :] = jnp.zeros((2, 8, 128), F32)

    def clear(i, c):
        for x in range(PASSES + 1):
            for f in range(4):
                stage[x, i // 2, f, lax.rem(i, 2), tail, :] = jnp.zeros((8, 128), F32)
        return c

    lax.fori_loop(0, 4, clear, 0)

    def extract(source, x, p):
        def one(i, c):
            n = 2 * p + i
            for v in range(NV):
                rows = pl.ds(FACE * v, FACE)
                stage[x, p, 0, i, rows, :] = source[v, n, pl.ds(0, FACE), :]
                stage[x, p, 1, i, rows, :] = source[v, n, pl.ds(100, FACE), :]
                for k in range(5):
                    stage[x, p, 2, i, pl.ds(FACE * v + 5 * k, 5), :] = source[v, n, pl.ds(25 * k, 5), :]
                    stage[x, p, 3, i, pl.ds(FACE * v + 5 * k, 5), :] = source[v, n, pl.ds(25 * k + 20, 5), :]
            return c

        lax.fori_loop(0, 2, one, 0)

    def send_faces(x, p):
        face_copy(x, p, 0).start()
        face_copy(x, p, 1).start()

        @pl.when(jnp.logical_not(at_bottom))
        def _():
            face_copy(x, p, 2).start()

        @pl.when(jnp.logical_not(at_top))
        def _():
            face_copy(x, p, 3).start()

    for p in range(2):
        extract(us, 0, p)

    pl.semaphore_wait(barrier, 6)

    @pl.when(outer)
    def _():
        for v in range(NV):
            raw_copy(v).start()

    for p in range(2):
        send_faces(0, p)

    diagonal = lax.broadcasted_iota(jnp.int32, (FACE, FACE), 0) == lax.broadcasted_iota(
        jnp.int32, (FACE, FACE), 1
    )
    for n in range(4):
        for v in range(NV):
            row = inflow_ref[n, pl.ds(v, 1), :]
            column = jnp.sum(jnp.where(diagonal, row, 0.0), axis=1, keepdims=True)
            inflow_cols[v, n, pl.ds(0, FACE), :] = jnp.broadcast_to(column, (FACE, 128))

    damping = []
    for d in range(3):
        sums = []
        for v in range(NV):
            total = jnp.abs(jac_ref[d, v, 0])
            for w in range(1, NV):
                total = total + jnp.abs(jac_ref[d, v, w])
            sums.append(total)
        largest = sums[0]
        for v in range(1, NV):
            largest = jnp.maximum(largest, sums[v])
        damping.append(largest)
    var_of = lax.broadcasted_iota(jnp.int32, (1, 128), 1) // FACE
    for v in range(NV):
        rows = pl.ds(ROWS * v, ROWS)
        low_rows = pl.ds(ROWS * (NV + v), ROWS)
        for w in range(NV):
            block = jac_ref[0, v, w] * pat_ref[0]
            for d in range(1, 3):
                block = block + jac_ref[d, v, w] * pat_ref[d]
            if v == w:
                for d in range(3):
                    block = block + damping[d] * pat_ref[3 + d]
            hi, lo = split(block)
            k_loc[rows, ROWS * w : ROWS * (w + 1)] = hi
            k_loc[low_rows, ROWS * w : ROWS * (w + 1)] = lo
        for f in range(6):
            d, side = f // 2, f % 2
            coef = jnp.zeros((1, 128), F32)
            for w in range(NV):
                value = jac_ref[d, v, w]
                if side == 0:
                    value = value - damping[d] if v == w else value
                else:
                    value = -(value + damping[d]) if v == w else -value
                coef = jnp.where(var_of == w, value, coef)
            hi, lo = split(pat_ref[6 + f] * coef)
            if f < 4:
                k_tr[rows, ROWS * f : ROWS * (f + 1)] = hi
                k_tr[low_rows, ROWS * f : ROWS * (f + 1)] = lo
            else:
                k_loc[rows, ROWS * (f + 1) : ROWS * (f + 2)] = hi
                k_loc[low_rows, ROWS * (f + 1) : ROWS * (f + 2)] = lo

    lane = lax.broadcasted_iota(jnp.int32, (FACE, 128), 1)

    def product(matrix, hi_ref, lo_ref):
        first = jnp.dot(matrix[...], hi_ref[...], preferred_element_type=F32)
        second = jnp.dot(matrix[pl.ds(0, ROWS * NV), :], lo_ref[...], preferred_element_type=F32)
        return first[: ROWS * NV] + first[ROWS * NV :] + second

    def local_part(source, p):
        for i in range(2):
            n = 2 * p + i
            cols = slice(128 * i, 128 * (i + 1))
            for v in range(NV):
                hi, lo = split(source[v, n])
                x_hi[pl.ds(ROWS * v, ROWS), cols] = hi
                x_lo[pl.ds(ROWS * v, ROWS), cols] = lo
                near = source[v, n, pl.ds(0, FACE, stride=5), :]
                far = source[v, n, pl.ds(4, FACE, stride=5), :]
                ax[0, pl.ds(FACE * v, FACE), :] = jnp.where(lane == 127, far, pltpu.roll(near, 127, 1))
                ax[1, pl.ds(FACE * v, FACE), :] = jnp.where(
                    lane == 0, inflow_cols[v, n, pl.ds(0, FACE), :], pltpu.roll(far, 1, 1)
                )
            for f in range(2):
                hi, lo = split(ax[f])
                x_hi[pl.ds(ROWS * (NV + f), ROWS), cols] = hi
                x_lo[pl.ds(ROWS * (NV + f), ROWS), cols] = lo
        total = product(k_loc, x_hi, x_lo)
        r[p, 0] = total[:, :128]
        r[p, 1] = total[:, 128:]

    row = lax.broadcasted_iota(jnp.int32, (ROWS, 128), 0)
    sign = jnp.where(jnp.logical_and(row >= 2 * FACE, row < 3 * FACE), -1.0, 1.0)

    def trace_part(x, p):
        def put(f, i, value):
            hi, lo = split(value)
            t_hi[pl.ds(ROWS * f, ROWS), 128 * i : 128 * (i + 1)] = hi
            t_lo[pl.ds(ROWS * f, ROWS), 128 * i : 128 * (i + 1)] = lo

        def arrived(f):
            face_copy(x, p, f).wait_recv()
            for i in range(2):
                put(f, i, faces[x, p, f, i])

        def mirrored(f):
            for i in range(2):
                put(f, i, sign * stage[x, p, 5 - f, i])

        for f, edge in ((2, at_top), (3, at_bottom)):
            pl.when(jnp.logical_not(edge))(functools.partial(arrived, f))
            pl.when(edge)(functools.partial(mirrored, f))
        for f in range(2):
            arrived(f)
        total = product(k_tr, t_hi, t_lo)
        r[p, 0] = r[p, 0] + total[:, :128]
        r[p, 1] = r[p, 1] + total[:, 128:]

    def finish(source, p):
        def one(i, c):
            inst = i // 4
            n = 2 * p + inst
            start = pl.multiple_of(lax.rem(i, 4) * CHUNK, CHUNK)
            rows = pl.ds(start, CHUNK)
            scale = metric[rows, :]
            values = [
                scale * r[p, inst, pl.ds(pl.multiple_of(ROWS * v + start, CHUNK), CHUNK), :] + spec[v, n, rows, :]
                for v in range(NV)
            ]
            for v in range(NV):
                total = pre_ref[n, pl.ds(NV * v, 1), :] * values[0]
                for w in range(1, NV):
                    total = total + pre_ref[n, pl.ds(NV * v + w, 1), :] * values[w]
                u[v, n, rows, :] = source[v, n, rows, :] - total
            return c

        lax.fori_loop(0, 8, one, 0)

    def results(p):
        for i in range(2):
            n = 2 * p + i
            for v in range(NV):
                rows = pl.ds(0, NODES)
                new_ref[n, v] = u[v, n, rows, :]
                res_ref[n, v] = metric[rows, :] * r[p, i, pl.ds(ROWS * v, NODES), :] + spec[v, n, rows, :]

    def weight(offset, n, m):
        return jnp.where(ahead, coupling(4 * offset + n - m), coupling(-4 * offset + n - m)).astype(F32)

    def send_cross(p, v):
        def one(c, carry):
            rows = pl.ds(pl.multiple_of(c * 16, 16), 16)
            mine = [us[v, m, rows, :] for m in range(4)]
            theirs = [raw[v, m, rows, :] for m in range(4)]
            for q in range(2):
                for i in range(2):
                    n = 2 * p + i
                    total = weight(1 + q, n, 0) * mine[0]
                    for m in range(1, 4):
                        total = total + weight(1 + q, n, m) * mine[m]
                    for m in range(4):
                        total = total + weight(2 + q, n, m) * theirs[m]
                    cross_out[p, v, q, i, rows, :] = total
            return carry

        lax.fori_loop(0, 8, one, 0)
        cross_copy(p, v).start()

    def inner_sums(p, v):
        cross_copy(p, v).wait_recv()

        def one(c, carry):
            rows = pl.ds(pl.multiple_of(c * 16, 16), 16)
            mine = [us[v, m, rows, :] for m in range(4)]
            theirs = [raw[v, m, rows, :] for m in range(4)]
            for i in range(2):
                n = 2 * p + i
                out = cross_in[p, v, 1, i, rows, :]
                own = cross_in[p, v, 0, i, rows, :]
                for m in range(4):
                    out = out + weight(-1, n, m) * mine[m]
                    if n != m:
                        own = own + coupling(n - m) * mine[m]
                    own = own + weight(1, n, m) * theirs[m]
                edge_out[p, v, i, rows, :] = out
                spec[v, n, rows, :] = own
            return carry

        lax.fori_loop(0, 8, one, 0)
        edge_copy(p, v).start()

    def outer_sums(p, v):
        edge_copy(p, v).wait_recv()

        def one(c, carry):
            rows = pl.ds(pl.multiple_of(c * 16, 16), 16)
            mine = [us[v, m, rows, :] for m in range(4)]
            for i in range(2):
                n = 2 * p + i
                own = edge_in[p, v, i, rows, :]
                for m in range(4):
                    if n != m:
                        own = own + coupling(n - m) * mine[m]
                spec[v, n, rows, :] = own
            return carry

        lax.fori_loop(0, 8, one, 0)

    def sums(p, variables):
        @pl.when(inner)
        def _():
            for v in variables:
                inner_sums(p, v)

        @pl.when(outer)
        def _():
            for v in variables:
                outer_sums(p, v)

    for p in range(2):
        local_part(us, p)

    @pl.when(inner)
    def _():
        for v in range(NV):
            raw_copy(v).wait_recv()
            send_cross(0, v)
        for v in range(NV):
            send_cross(1, v)

    for p in range(2):
        trace_part(0, p)

    def advance(source, x, p):
        finish(source, p)
        extract(u, x + 1, p)
        send_faces(x + 1, p)
        local_part(u, p)

    sums(0, range(NV))
    advance(us, 0, 0)
    sums(1, (0, 1))
    trace_part(1, 0)
    advance(u, 1, 0)
    sums(1, (2, 3))
    trace_part(2, 0)
    advance(u, 2, 0)
    sums(1, (4,))
    advance(us, 0, 1)
    trace_part(3, 0)
    results(0)
    trace_part(1, 1)
    advance(u, 1, 1)
    trace_part(2, 1)
    advance(u, 2, 1)
    trace_part(3, 1)
    results(1)

    for x in range(PASSES + 1):
        for p in range(2):
            face_copy(x, p, 0).wait_send()
            face_copy(x, p, 1).wait_send()

            @pl.when(jnp.logical_not(at_bottom))
            def _(x=x, p=p):
                face_copy(x, p, 2).wait_send()

            @pl.when(jnp.logical_not(at_top))
            def _(x=x, p=p):
                face_copy(x, p, 3).wait_send()

    @pl.when(outer)
    def _():
        for v in range(NV):
            raw_copy(v).wait_send()

    @pl.when(inner)
    def _():
        for p in range(2):
            for v in range(NV):
                cross_copy(p, v).wait_send()
                edge_copy(p, v).wait_send()


def per_device(state, metric_scale, flux_jacobians, preconditioner, inflow):
    vmem = pl.BlockSpec(memory_space=pltpu.VMEM)
    smem = pl.BlockSpec(memory_space=pltpu.SMEM)
    block = (4, NV, NODES, 128)
    dma = pltpu.SemaphoreType.DMA
    exchanges = PASSES + 1
    new_state, residual = pl.pallas_call(
        kernel,
        name="pseudo_step",
        out_shape=(jax.ShapeDtypeStruct(block, F32), jax.ShapeDtypeStruct(block, F32)),
        in_specs=[vmem, vmem, smem, vmem, vmem, vmem],
        out_specs=(vmem, vmem),
        scratch_shapes=[
            pltpu.VMEM((NV, 4, ROWS, 128), F32),
            pltpu.VMEM((NV, 4, ROWS, 128), F32),
            pltpu.VMEM((NV, 4, ROWS, 128), F32),
            pltpu.VMEM((ROWS, 128), F32),
            pltpu.VMEM((NV, 4, 32, 128), F32),
            pltpu.VMEM((2 * NV * ROWS, 7 * ROWS), BF16),
            pltpu.VMEM((2 * NV * ROWS, 4 * ROWS), BF16),
            pltpu.VMEM((7 * ROWS, 256), BF16),
            pltpu.VMEM((7 * ROWS, 256), BF16),
            pltpu.VMEM((4 * ROWS, 256), BF16),
            pltpu.VMEM((4 * ROWS, 256), BF16),
            pltpu.VMEM((2, 2, NV * ROWS, 128), F32),
            pltpu.VMEM((2, ROWS, 128), F32),
            pltpu.VMEM((exchanges, 2, 4, 2, ROWS, 128), F32),
            pltpu.VMEM((exchanges, 2, 4, 2, ROWS, 128), F32),
            pltpu.VMEM((NV, 4, ROWS, 128), F32),
            pltpu.VMEM((2, NV, 2, 2, ROWS, 128), F32),
            pltpu.VMEM((2, NV, 2, 2, ROWS, 128), F32),
            pltpu.VMEM((2, NV, 2, ROWS, 128), F32),
            pltpu.VMEM((2, NV, 2, ROWS, 128), F32),
            dma((exchanges, 2, 4)),
            dma((exchanges, 2, 4)),
            dma((NV,)),
            dma((NV,)),
            dma((2, NV)),
            dma((2, NV)),
            dma((2, NV)),
            dma((2, NV)),
        ],
        compiler_params=pltpu.CompilerParams(
            collective_id=0, has_side_effects=True, vmem_limit_bytes=60 * 2**20
        ),
    )(
        state.reshape(block),
        metric_scale.reshape(NODES, 128),
        flux_jacobians,
        preconditioner.reshape(4, NV * NV, 128),
        inflow.reshape(4, NV, FACE),
        jnp.asarray(patterns()),
    )
    return new_state.reshape(state.shape), residual.reshape(state.shape)


def solution(mesh):
    in_specs = (
        P("tm", None, "elem", None, None),
        P("elem", None, None),
        P(),
        P("tm", None, None, "elem", None),
        P("tm", None, "elem", None),
    )
    out_specs = (P("tm", None, "elem", None, None), P("tm", None, "elem", None, None))
    return jax.shard_map(
        per_device, mesh=mesh, in_specs=in_specs, out_specs=out_specs, check_vma=False
    )
```

```python
import functools
import math

import jax
import jax.numpy as jnp
import numpy as np
from jax import lax
from jax.experimental import pallas as pl
from jax.experimental.pallas import tpu as pltpu
from jax.sharding import PartitionSpec as P

NI = 16
NV = 5
PR = 8
PASSES = 3
ROWS = 128
NODES = 125
FACE = 25
CHUNK = 32
GROUPS = ((0, 2), (2, 1), (3, 1))
WHOLE = 2
VIA = ((0, 1), (0, 1), (0, 1))
MESH = pl.DeviceIdType.MESH
F32 = jnp.float32
BF16 = jnp.bfloat16


def gll_derivative():
    points = np.array([-1.0, -math.sqrt(3.0 / 7.0), 0.0, math.sqrt(3.0 / 7.0), 1.0])
    legendre = (35.0 * points**4 - 30.0 * points**2 + 3.0) / 8.0
    identity = np.eye(5, dtype=bool)
    spacing = np.where(identity, 1.0, points[:, None] - points[None, :])
    matrix = legendre[:, None] / legendre[None, :] / spacing
    corner = np.array([-5.0, 0.0, 0.0, 0.0, 5.0])[None, :]
    return np.where(identity, corner, matrix)


def coupling(offset):
    if offset % NI == 0:
        return 0.0
    angle = math.pi * offset / NI
    return 0.5 * (1.0 - 2.0 * (offset % 2)) * math.cos(angle) / math.sin(angle)


def patterns():
    table = gll_derivative()
    node = np.arange(NODES)
    index = [node // 25, (node // 5) % 5, node % 5]
    out = np.zeros((12, ROWS, ROWS))
    for d in range(3):
        others = [index[o] for o in range(3) if o != d]
        same = np.ones((NODES, NODES), bool)
        for o in others:
            same &= o[:, None] == o[None, :]
        out[d, :NODES, :NODES] = np.where(same, table[index[d][:, None], index[d][None, :]], 0.0)
        high, low = index[d] == 4, index[d] == 0
        out[d, node, node] += np.where(high, -5.0, 0.0) + np.where(low, 5.0, 0.0)
        out[3 + d, node, node] = np.where(high | low, 5.0, 0.0)
        for side, face in enumerate((high, low)):
            dest = node[face]
            for v in range(NV):
                out[6 + 2 * d + side, dest, FACE * v + np.arange(FACE)] = 5.0
    return out.astype(np.float32)


def split(value):
    high = value.astype(BF16)
    low = (value - high.astype(F32)).astype(BF16)
    return high, low


def kernel(
    state_ref, metric_ref, jac_ref, pre_ref, inflow_ref, pat_ref, new_ref, res_ref,
    us, u, spec, res, metric, pre, inflow_cols, k_loc, k_tr, x_hi, x_lo, t_hi, t_lo, r, ax,
    stage, faces, passing, raw, near_in, far_in, cross_out, cross_in, edge_out, edge_in,
    face_s, face_r, via_s, via_r, on_s, raw_s, raw_r, near_s, near_r, far_s, far_r, cross_s, cross_r, edge_s, edge_r, in_s, out_s,
):
    t = lax.axis_index("tm")
    e = lax.axis_index("elem")
    inner = jnp.logical_or(t == 1, t == 2)
    outer = jnp.logical_not(inner)
    ahead = t < 2
    beside = jnp.where(inner, jnp.where(t == 1, 0, 3), jnp.where(t == 0, 1, 2))
    opposite = jnp.where(inner, 3 - t, t)
    at_top = lax.rem(e, PR) == PR // 2 - 1
    at_bottom = lax.rem(e, PR) == PR // 2
    following = lax.rem(e + PR, 64)
    preceding = lax.rem(e + 64 - PR, 64)
    above = lax.rem(e + 1, 64)
    below = lax.rem(e + 63, 64)

    core, x_of, in_half = lax.rem(e, 2), lax.rem(e // 8, 4), lax.rem(e, 32)
    y_of = lax.rem(e // 2, 4)

    def at(x, y):
        return jnp.logical_and(jnp.logical_and(x_of == x, y_of == y), core == 1)

    routes = ((at(0, 0), at(1, 0), at(3, 0), -16), (at(3, 3), at(2, 3), at(0, 3), 16))
    used = [f for f in range(4) if any(f in faces_of for faces_of in VIA)]

    barrier = pltpu.get_barrier_semaphore()
    for peer in (following, preceding, above, below):
        pl.semaphore_signal(barrier, inc=1, device_id=(t, peer), device_id_type=MESH)
    for step in (1, 2, 3):
        pl.semaphore_signal(barrier, inc=1, device_id=(lax.rem(t + step, 4), e), device_id_type=MESH)

    for f in used:
        @pl.when(routes[f][2])
        def _(f=f):
            relay = lax.rem(e + 64 - routes[f][3], 64)
            pl.semaphore_signal(barrier, inc=1, device_id=(t, relay), device_id_type=MESH)

    def remote(source, target, send, recv, peer_t, peer_e):
        return pltpu.make_async_remote_copy(
            src_ref=source, dst_ref=target, send_sem=send, recv_sem=recv,
            device_id=(peer_t, peer_e), device_id_type=MESH,
        )

    def members(g):
        return pl.ds(GROUPS[g][0], GROUPS[g][1])

    def face_copy(x, g, f):
        peer = (preceding, following, below, above)[f]
        part = (x, f, members(g))
        return remote(stage.at[part], faces.at[part], face_s.at[x, g, f], face_r.at[x, g, f], t, peer)

    def via_copy(x, g, f):
        peer = (following, preceding)[f % 2]
        part = (x, f, members(g))
        return remote(stage.at[part], passing.at[part], via_s.at[x, g, f], via_r.at[x, g, f], t, peer)

    def on_copy(x, g, f):
        part = (x, f, members(g))
        peer = lax.rem(e + 64 + routes[f][3], 64)
        return remote(passing.at[part], faces.at[part], on_s.at[x, g, f], face_r.at[x, g, f], t, peer)

    def sending(x, g, f, act):
        wall = (None, None, at_bottom, at_top)[f]
        straight = None if wall is None else jnp.logical_not(wall)
        if f in VIA[g]:
            first = routes[f][0]
            rest = jnp.logical_not(first)
            straight = rest if straight is None else jnp.logical_and(straight, rest)
            pl.when(first)(lambda: act(via_copy(x, g, f)))
        if straight is None:
            act(face_copy(x, g, f))
        else:
            pl.when(straight)(lambda: act(face_copy(x, g, f)))

    def pass_on(x, g):
        for f in VIA[g]:

            @pl.when(routes[f][1])
            def _(f=f):
                via_copy(x, g, f).wait_recv()
                on_copy(x, g, f).start()

    def raw_copy(v):
        return remote(us.at[v], raw.at[v], raw_s.at[v], raw_r.at[v], beside, e)

    def near_copy(v):
        return remote(us.at[v], near_in.at[v], near_s.at[v], near_r.at[v], opposite, e)

    def far_copy(v):
        return remote(us.at[v], far_in.at[v], far_s.at[v], far_r.at[v], lax.rem(t + 2, 4), e)

    def cross_copy(g, v):
        part = (v, members(g))
        return remote(cross_out.at[part], cross_in.at[part], cross_s.at[g, v], cross_r.at[g, v], opposite, e)

    def edge_copy(g, v):
        part = (v, members(g))
        return remote(edge_out.at[part], edge_in.at[part], edge_s.at[g, v], edge_r.at[g, v], beside, e)

    nodes = pl.ds(0, NODES)
    loads = [
        pltpu.make_async_copy(state_ref.at[n, v, :, 0, :], us.at[v, n, nodes, :], in_s.at[v, n])
        for n in range(4)
        for v in range(NV)
    ]
    loads.append(pltpu.make_async_copy(metric_ref.at[:, 0, :], metric.at[nodes, :], in_s.at[NV, 0]))
    for n in range(4):
        loads.append(pltpu.make_async_copy(pre_ref.at[n, :, 0, :], pre.at[n], in_s.at[NV + 1, n]))
    for load in loads:
        load.start()
    last = pl.ds(NODES, ROWS - NODES)
    tail = pl.ds(ROWS - 8, 8)
    metric[last, :] = jnp.zeros((3, 128), F32)
    for v in range(NV):
        for n in range(4):
            us[v, n, last, :] = jnp.zeros((3, 128), F32)
    ax[:, tail, :] = jnp.zeros((2, 8, 128), F32)

    def clear(n, c):
        for x in range(PASSES + 1):
            for f in range(4):
                stage[x, f, n, tail, :] = jnp.zeros((8, 128), F32)
        return c

    lax.fori_loop(0, 4, clear, 0)

    def extract(source, x, g):
        def one(i, c):
            n = GROUPS[g][0] + i
            for v in range(NV):
                rows = pl.ds(FACE * v, FACE)
                stage[x, 0, n, rows, :] = source[v, n, pl.ds(0, FACE), :]
                stage[x, 1, n, rows, :] = source[v, n, pl.ds(100, FACE), :]
                for k in range(5):
                    stage[x, 2, n, pl.ds(FACE * v + 5 * k, 5), :] = source[v, n, pl.ds(25 * k, 5), :]
                    stage[x, 3, n, pl.ds(FACE * v + 5 * k, 5), :] = source[v, n, pl.ds(25 * k + 20, 5), :]
            return c

        lax.fori_loop(0, GROUPS[g][1], one, 0)

    def send_faces(x, g):
        for f in (0, 1, 2, 3):
            sending(x, g, f, lambda copy: copy.start())

    for load in loads:
        load.wait()

    expected = 7
    for f in used:
        expected = expected + jnp.where(routes[f][1], 1, 0)
    pl.semaphore_wait(barrier, expected)

    @pl.when(outer)
    def _():
        order = []
        for v in range(WHOLE, NV):
            order.append(raw_copy(v))
            if v - WHOLE < WHOLE:
                order.append(far_copy(v - WHOLE))
        for v in range(NV - WHOLE, WHOLE):
            order.append(far_copy(v))
        for v in range(WHOLE):
            order.append(raw_copy(v))
        for copy in order:
            copy.start()

    @pl.when(inner)
    def _():
        for v in range(WHOLE):
            near_copy(v).start()

    for g in range(len(GROUPS)):
        extract(us, 0, g)
        send_faces(0, g)

    diagonal = lax.broadcasted_iota(jnp.int32, (FACE, FACE), 0) == lax.broadcasted_iota(
        jnp.int32, (FACE, FACE), 1
    )
    for n in range(4):
        for v in range(NV):
            row = inflow_ref[n, v]
            column = jnp.sum(jnp.where(diagonal, row, 0.0), axis=1, keepdims=True)
            inflow_cols[v, n, pl.ds(0, FACE), :] = jnp.broadcast_to(column, (FACE, 128))

    damping = []
    for d in range(3):
        sums = []
        for v in range(NV):
            total = jnp.abs(jac_ref[v, d, 0])
            for w in range(1, NV):
                total = total + jnp.abs(jac_ref[v, d, w])
            sums.append(total)
        largest = sums[0]
        for v in range(1, NV):
            largest = jnp.maximum(largest, sums[v])
        damping.append(largest)
    var_of = lax.broadcasted_iota(jnp.int32, (1, 128), 1) // FACE
    for v in range(NV):
        rows = pl.ds(ROWS * v, ROWS)
        low_rows = pl.ds(ROWS * (NV + v), ROWS)
        for w in range(NV):
            block = jac_ref[v, 0, w] * pat_ref[0]
            for d in range(1, 3):
                block = block + jac_ref[v, d, w] * pat_ref[d]
            if v == w:
                for d in range(3):
                    block = block + damping[d] * pat_ref[3 + d]
            hi, lo = split(block)
            k_loc[rows, ROWS * w : ROWS * (w + 1)] = hi
            k_loc[low_rows, ROWS * w : ROWS * (w + 1)] = lo
        for f in range(6):
            d, side = f // 2, f % 2
            coef = jnp.zeros((1, 128), F32)
            for w in range(NV):
                value = jac_ref[v, d, w]
                if side == 0:
                    value = value - damping[d] if v == w else value
                else:
                    value = -(value + damping[d]) if v == w else -value
                coef = jnp.where(var_of == w, value, coef)
            hi, lo = split(pat_ref[6 + f] * coef)
            if f < 4:
                k_tr[rows, ROWS * f : ROWS * (f + 1)] = hi
                k_tr[low_rows, ROWS * f : ROWS * (f + 1)] = lo
            else:
                k_loc[rows, ROWS * (f + 1) : ROWS * (f + 2)] = hi
                k_loc[low_rows, ROWS * (f + 1) : ROWS * (f + 2)] = lo

    lane = lax.broadcasted_iota(jnp.int32, (FACE, 128), 1)

    def product(matrix, hi, lo):
        first = jnp.dot(matrix[...], hi, preferred_element_type=F32)
        second = jnp.dot(matrix[pl.ds(0, ROWS * NV), :], lo, preferred_element_type=F32)
        return first[: ROWS * NV] + first[ROWS * NV :] + second

    def local_part(source, g):
        first, count = GROUPS[g]
        for i in range(count):
            n = first + i
            cols = slice(128 * i, 128 * (i + 1))
            for v in range(NV):
                hi, lo = split(source[v, n])
                x_hi[pl.ds(ROWS * v, ROWS), cols] = hi
                x_lo[pl.ds(ROWS * v, ROWS), cols] = lo
                near = source[v, n, pl.ds(0, FACE, stride=5), :]
                far = source[v, n, pl.ds(4, FACE, stride=5), :]
                ax[0, pl.ds(FACE * v, FACE), :] = jnp.where(lane == 127, far, pltpu.roll(near, 127, 1))
                ax[1, pl.ds(FACE * v, FACE), :] = jnp.where(
                    lane == 0, inflow_cols[v, n, pl.ds(0, FACE), :], pltpu.roll(far, 1, 1)
                )
            for f in range(2):
                hi, lo = split(ax[f])
                x_hi[pl.ds(ROWS * (NV + f), ROWS), cols] = hi
                x_lo[pl.ds(ROWS * (NV + f), ROWS), cols] = lo
        used = slice(0, 128 * count)
        total = product(k_loc, x_hi[:, used], x_lo[:, used])
        for i in range(count):
            r[first + i] = total[:, 128 * i : 128 * (i + 1)]

    row = lax.broadcasted_iota(jnp.int32, (ROWS, 128), 0)
    sign = jnp.where(jnp.logical_and(row >= 2 * FACE, row < 3 * FACE), -1.0, 1.0)

    def trace_part(x, g):
        first, count = GROUPS[g]

        def put(f, i, value):
            hi, lo = split(value)
            t_hi[pl.ds(ROWS * f, ROWS), 128 * i : 128 * (i + 1)] = hi
            t_lo[pl.ds(ROWS * f, ROWS), 128 * i : 128 * (i + 1)] = lo

        def arrived(f):
            face_copy(x, g, f).wait_recv()
            for i in range(count):
                put(f, i, faces[x, f, first + i])

        def mirrored(f):
            for i in range(count):
                put(f, i, sign * stage[x, 5 - f, first + i])

        for f, edge in ((2, at_top), (3, at_bottom)):
            pl.when(jnp.logical_not(edge))(functools.partial(arrived, f))
            pl.when(edge)(functools.partial(mirrored, f))
        for f in range(2):
            arrived(f)
        used = slice(0, 128 * count)
        total = product(k_tr, t_hi[:, used], t_lo[:, used])
        for i in range(count):
            r[first + i] = r[first + i] + total[:, 128 * i : 128 * (i + 1)]

    def finish(source, g):
        first, count = GROUPS[g]

        def one(i, c):
            n = first + i // 4
            start = pl.multiple_of(lax.rem(i, 4) * CHUNK, CHUNK)
            rows = pl.ds(start, CHUNK)
            scale = metric[rows, :]
            values = [
                scale * r[n, pl.ds(pl.multiple_of(ROWS * v + start, CHUNK), CHUNK), :] + spec[v, n, rows, :]
                for v in range(NV)
            ]
            for v in range(NV):
                total = pre[n, pl.ds(NV * v, 1), :] * values[0]
                for w in range(1, NV):
                    total = total + pre[n, pl.ds(NV * v + w, 1), :] * values[w]
                u[v, n, rows, :] = source[v, n, rows, :] - total
            return c

        lax.fori_loop(0, 4 * count, one, 0)

    def stores(g, kind):
        buffer, target = ((u, new_ref), (res, res_ref))[kind]
        first, count = GROUPS[g]
        return [
            pltpu.make_async_copy(buffer.at[v, n, nodes, :], target.at[n, v, :, 0, :], out_s.at[kind, v, n])
            for n in range(first, first + count)
            for v in range(NV)
        ]

    def results(g):
        first, count = GROUPS[g]
        for n in range(first, first + count):
            for v in range(NV):
                res[v, n] = metric[...] * r[n, pl.ds(ROWS * v, ROWS), :] + spec[v, n]
        for store in stores(g, 1):
            store.start()

    def weight(offset, n, m):
        return jnp.where(ahead, coupling(4 * offset + n - m), coupling(-4 * offset + n - m)).astype(F32)

    def tiles(body):
        def one(c, carry):
            body(pl.ds(pl.multiple_of(c * 16, 16), 16))
            return carry

        lax.fori_loop(0, 8, one, 0)

    def combine(total, offset, n, values):
        for m in range(4):
            total = total + weight(offset, n, m) * values[m]
        return total

    def own_part(total, n, values):
        for m in range(4):
            if n != m:
                total = total + coupling(n - m) * values[m]
        return total

    def instances(g):
        return range(GROUPS[g][0], GROUPS[g][0] + GROUPS[g][1])

    def send_cross(g, v):
        def body(rows):
            mine = [us[v, m, rows, :] for m in range(4)]
            theirs = [raw[v, m, rows, :] for m in range(4)]
            for n in instances(g):
                for q in range(2):
                    total = combine(jnp.zeros((16, 128), F32), 1 + q, n, mine)
                    cross_out[v, n, q, rows, :] = combine(total, 2 + q, n, theirs)

        tiles(body)
        cross_copy(g, v).start()

    def whole_sums(v):
        raw_copy(v).wait_recv()
        near_copy(v).wait_recv()
        far_copy(v).wait_recv()

        def body(rows):
            mine = [us[v, m, rows, :] for m in range(4)]
            theirs = [raw[v, m, rows, :] for m in range(4)]
            near = [near_in[v, m, rows, :] for m in range(4)]
            far = [far_in[v, m, rows, :] for m in range(4)]
            for n in range(4):
                zero = jnp.zeros((16, 128), F32)
                edge_out[v, n, rows, :] = combine(combine(combine(zero, -1, n, mine), -2, n, near), -3, n, far)
                spec[v, n, rows, :] = combine(
                    combine(combine(own_part(zero, n, mine), 1, n, theirs), -1, n, near), -2, n, far
                )

        tiles(body)
        edge_copy(0, v).start()

    def inner_sums(g, v):
        cross_copy(g, v).wait_recv()

        def body(rows):
            mine = [us[v, m, rows, :] for m in range(4)]
            theirs = [raw[v, m, rows, :] for m in range(4)]
            for n in instances(g):
                edge_out[v, n, rows, :] = combine(cross_in[v, n, 1, rows, :], -1, n, mine)
                spec[v, n, rows, :] = combine(own_part(cross_in[v, n, 0, rows, :], n, mine), 1, n, theirs)

        tiles(body)
        edge_copy(g, v).start()

    def outer_sums(g, v):
        edge_copy(g, v).wait_recv()

        def body(rows):
            mine = [us[v, m, rows, :] for m in range(4)]
            for n in instances(g):
                spec[v, n, rows, :] = own_part(edge_in[v, n, rows, :], n, mine)

        tiles(body)

    def sums(g):
        @pl.when(inner)
        def _():
            for v in range(WHOLE, NV):
                inner_sums(g, v)

        @pl.when(outer)
        def _():
            for v in range(NV):
                outer_sums(g, v)

    def advance(source, x, g):
        finish(source, g)
        extract(u, x + 1, g)
        send_faces(x + 1, g)
        if x == PASSES - 1:
            for store in stores(g, 0):
                store.start()
        local_part(u, g)
        pass_on(x + 1, g)

    for g in range(len(GROUPS)):
        local_part(us, g)
    for g in range(len(GROUPS)):
        pass_on(0, g)

    @pl.when(inner)
    def _():
        for v in range(WHOLE, NV):
            raw_copy(v).wait_recv()
            send_cross(0, v)
            if v > WHOLE:
                inner_sums(0, v - 1)
        for g in range(1, len(GROUPS)):
            for v in range(WHOLE, NV):
                send_cross(g, v)
        for v in range(WHOLE):
            whole_sums(v)
        inner_sums(0, NV - 1)
        for g in range(1, len(GROUPS)):
            for v in range(WHOLE):
                edge_copy(g, v).start()

    for g in range(len(GROUPS)):
        trace_part(0, g)

    @pl.when(outer)
    def _():
        for v in (*range(WHOLE, NV - 1), *range(WHOLE), NV - 1):
            outer_sums(0, v)

    advance(us, 0, 0)
    sums(1)
    advance(us, 0, 1)
    trace_part(1, 0)
    advance(u, 1, 0)
    sums(2)
    advance(us, 0, 2)
    trace_part(1, 1)
    advance(u, 1, 1)
    trace_part(2, 0)
    advance(u, 2, 0)
    trace_part(1, 2)
    advance(u, 1, 2)
    trace_part(2, 1)
    advance(u, 2, 1)
    trace_part(3, 0)
    results(0)
    trace_part(2, 2)
    advance(u, 2, 2)
    trace_part(3, 1)
    results(1)
    trace_part(3, 2)
    results(2)

    for g in range(len(GROUPS)):
        for kind in range(2):
            for store in stores(g, kind):
                store.wait()

    for g in range(len(GROUPS)):
        for x in range(PASSES + 1):
            for f in range(4):
                sending(x, g, f, lambda copy: copy.wait_send())
            for f in VIA[g]:

                @pl.when(routes[f][1])
                def _(x=x, g=g, f=f):
                    on_copy(x, g, f).wait_send()

    @pl.when(outer)
    def _():
        for v in range(NV):
            raw_copy(v).wait_send()
        for v in range(WHOLE):
            far_copy(v).wait_send()

    @pl.when(inner)
    def _():
        for v in range(WHOLE):
            near_copy(v).wait_send()
        for g in range(len(GROUPS)):
            for v in range(NV):
                if v >= WHOLE:
                    cross_copy(g, v).wait_send()
                edge_copy(g, v).wait_send()


def per_device(state, metric_scale, flux_jacobians, preconditioner, inflow):
    vmem = pl.BlockSpec(memory_space=pltpu.VMEM)
    smem = pl.BlockSpec(memory_space=pltpu.SMEM)
    block = (4, NV, NODES, 1, 128)
    hbm = pl.BlockSpec(memory_space=pl.ANY)
    dma = pltpu.SemaphoreType.DMA
    exchanges = PASSES + 1
    groups = len(GROUPS)
    new_state, residual = pl.pallas_call(
        kernel,
        name="pseudo_step",
        out_shape=(jax.ShapeDtypeStruct(block, F32), jax.ShapeDtypeStruct(block, F32)),
        in_specs=[hbm, hbm, smem, hbm, vmem, vmem],
        out_specs=(hbm, hbm),
        scratch_shapes=[
            pltpu.VMEM((NV, 4, ROWS, 128), F32),
            pltpu.VMEM((NV, 4, ROWS, 128), F32),
            pltpu.VMEM((NV, 4, ROWS, 128), F32),
            pltpu.VMEM((NV, 4, ROWS, 128), F32),
            pltpu.VMEM((ROWS, 128), F32),
            pltpu.VMEM((4, NV * NV, 128), F32),
            pltpu.VMEM((NV, 4, 32, 128), F32),
            pltpu.VMEM((2 * NV * ROWS, 7 * ROWS), BF16),
            pltpu.VMEM((2 * NV * ROWS, 4 * ROWS), BF16),
            pltpu.VMEM((7 * ROWS, 256), BF16),
            pltpu.VMEM((7 * ROWS, 256), BF16),
            pltpu.VMEM((4 * ROWS, 256), BF16),
            pltpu.VMEM((4 * ROWS, 256), BF16),
            pltpu.VMEM((4, NV * ROWS, 128), F32),
            pltpu.VMEM((2, ROWS, 128), F32),
            pltpu.VMEM((exchanges, 4, 4, ROWS, 128), F32),
            pltpu.VMEM((exchanges, 4, 4, ROWS, 128), F32),
            pltpu.VMEM((exchanges, 4, 4, ROWS, 128), F32),
            pltpu.VMEM((NV, 4, ROWS, 128), F32),
            pltpu.VMEM((WHOLE, 4, ROWS, 128), F32),
            pltpu.VMEM((WHOLE, 4, ROWS, 128), F32),
            pltpu.VMEM((NV, 4, 2, ROWS, 128), F32),
            pltpu.VMEM((NV, 4, 2, ROWS, 128), F32),
            pltpu.VMEM((NV, 4, ROWS, 128), F32),
            pltpu.VMEM((NV, 4, ROWS, 128), F32),
            dma((exchanges, groups, 4)),
            dma((exchanges, groups, 4)),
            dma((exchanges, groups, 4)),
            dma((exchanges, groups, 4)),
            dma((exchanges, groups, 4)),
            dma((NV,)),
            dma((NV,)),
            dma((WHOLE,)),
            dma((WHOLE,)),
            dma((WHOLE,)),
            dma((WHOLE,)),
            dma((groups, NV)),
            dma((groups, NV)),
            dma((groups, NV)),
            dma((groups, NV)),
            dma((NV + 2, 4)),
            dma((2, NV, 4)),
        ],
        compiler_params=pltpu.CompilerParams(
            collective_id=0, has_side_effects=True, vmem_limit_bytes=60 * 2**20
        ),
    )(
        state.reshape(block),
        metric_scale.reshape(NODES, 1, 128),
        flux_jacobians.transpose(1, 0, 2),
        preconditioner.reshape(4, NV * NV, 1, 128),
        inflow.reshape(4, NV, 1, FACE),
        jnp.asarray(patterns()),
    )
    return new_state.reshape(state.shape), residual.reshape(state.shape)


def solution(mesh):
    in_specs = (
        P("tm", None, "elem", None, None),
        P("elem", None, None),
        P(),
        P("tm", None, None, "elem", None),
        P("tm", None, "elem", None),
    )
    out_specs = (P("tm", None, "elem", None, None), P("tm", None, "elem", None, None))
    return jax.shard_map(
        per_device, mesh=mesh, in_specs=in_specs, out_specs=out_specs, check_vma=False
    )
```

```python
import functools
import math

import jax
import jax.numpy as jnp
import numpy as np
from jax import lax
from jax.experimental import pallas as pl
from jax.experimental.pallas import tpu as pltpu
from jax.sharding import PartitionSpec as P

NI = 16
NV = 5
PR = 8
PASSES = 3
ROWS = 128
NODES = 125
FACE = 25
CHUNK = 32
GROUPS = ((0, 2), (2, 1), (3, 1))
WHOLE = 2
MESH = pl.DeviceIdType.MESH
F32 = jnp.float32
BF16 = jnp.bfloat16


def gll_derivative():
    points = np.array([-1.0, -math.sqrt(3.0 / 7.0), 0.0, math.sqrt(3.0 / 7.0), 1.0])
    legendre = (35.0 * points**4 - 30.0 * points**2 + 3.0) / 8.0
    identity = np.eye(5, dtype=bool)
    spacing = np.where(identity, 1.0, points[:, None] - points[None, :])
    matrix = legendre[:, None] / legendre[None, :] / spacing
    corner = np.array([-5.0, 0.0, 0.0, 0.0, 5.0])[None, :]
    return np.where(identity, corner, matrix)


def coupling(offset):
    if offset % NI == 0:
        return 0.0
    angle = math.pi * offset / NI
    return 0.5 * (1.0 - 2.0 * (offset % 2)) * math.cos(angle) / math.sin(angle)


def patterns():
    table = gll_derivative()
    node = np.arange(NODES)
    index = [node // 25, (node // 5) % 5, node % 5]
    out = np.zeros((12, ROWS, ROWS))
    for d in range(3):
        others = [index[o] for o in range(3) if o != d]
        same = np.ones((NODES, NODES), bool)
        for o in others:
            same &= o[:, None] == o[None, :]
        out[d, :NODES, :NODES] = np.where(same, table[index[d][:, None], index[d][None, :]], 0.0)
        high, low = index[d] == 4, index[d] == 0
        out[d, node, node] += np.where(high, -5.0, 0.0) + np.where(low, 5.0, 0.0)
        out[3 + d, node, node] = np.where(high | low, 5.0, 0.0)
        for side, face in enumerate((high, low)):
            dest = node[face]
            for v in range(NV):
                out[6 + 2 * d + side, dest, FACE * v + np.arange(FACE)] = 5.0
    return out.astype(np.float32)


def split(value):
    high = value.astype(BF16)
    low = (value - high.astype(F32)).astype(BF16)
    return high, low


def kernel(
    state_ref, metric_ref, jac_ref, pre_ref, inflow_ref, pat_ref, new_ref, res_ref,
    us, u, spec, res, metric, pre, inflow_cols, k_loc, k_tr, x_hi, x_lo, t_hi, t_lo, r, ax,
    stage, faces, passing, raw, near_in, far_in, cross_out, cross_in, edge_out, edge_in,
    face_s, face_r, via_s, via_r, on_s, raw_s, raw_r, near_s, near_r, far_s, far_r, cross_s, cross_r, edge_s, edge_r, in_s, out_s,
):
    t = lax.axis_index("tm")
    e = lax.axis_index("elem")
    inner = jnp.logical_or(t == 1, t == 2)
    outer = jnp.logical_not(inner)
    ahead = t < 2
    beside = jnp.where(inner, jnp.where(t == 1, 0, 3), jnp.where(t == 0, 1, 2))
    opposite = jnp.where(inner, 3 - t, t)
    at_top = lax.rem(e, PR) == PR // 2 - 1
    at_bottom = lax.rem(e, PR) == PR // 2
    following = lax.rem(e + PR, 64)
    preceding = lax.rem(e + 64 - PR, 64)
    above = lax.rem(e + 1, 64)
    below = lax.rem(e + 63, 64)

    core, x_of, y_of = lax.rem(e, 2), lax.rem(e // 8, 4), lax.rem(e // 2, 4)

    def at(x):
        return jnp.logical_and(x_of == x, core == 1)

    def route(f, x):
        edge, relay, other, distance, row = ((0, 1, 3, -16, 3), (3, 2, 0, 16, 0))[f]
        places = [at(edge), at(relay), at(other)]
        if x >= 2:
            places = [jnp.logical_and(place, y_of != row) for place in places]
        return (*places, distance)

    barrier = pltpu.get_barrier_semaphore()
    for peer in (following, preceding, above, below):
        pl.semaphore_signal(barrier, inc=1, device_id=(t, peer), device_id_type=MESH)
    for step in (1, 2, 3):
        pl.semaphore_signal(barrier, inc=1, device_id=(lax.rem(t + step, 4), e), device_id_type=MESH)

    for f in range(2):
        _, _, last_device, distance = route(f, 0)

        @pl.when(last_device)
        def _(distance=distance):
            relay = lax.rem(e + 64 - distance, 64)
            pl.semaphore_signal(barrier, inc=1, device_id=(t, relay), device_id_type=MESH)

    def remote(source, target, send, recv, peer_t, peer_e):
        return pltpu.make_async_remote_copy(
            src_ref=source, dst_ref=target, send_sem=send, recv_sem=recv,
            device_id=(peer_t, peer_e), device_id_type=MESH,
        )

    def members(g):
        return pl.ds(GROUPS[g][0], GROUPS[g][1])

    def face_copy(x, g, f):
        peer = (preceding, following, below, above)[f]
        part = (x, f, members(g))
        return remote(stage.at[part], faces.at[part], face_s.at[x, g, f], face_r.at[x, g, f], t, peer)

    def via_copy(x, g, f):
        peer = (following, preceding)[f % 2]
        part = (x, f, members(g))
        return remote(stage.at[part], passing.at[part], via_s.at[x, g, f], via_r.at[x, g, f], t, peer)

    def on_copy(x, g, f):
        part = (x, f, members(g))
        peer = lax.rem(e + 64 + route(f, x)[3], 64)
        return remote(passing.at[part], faces.at[part], on_s.at[x, g, f], face_r.at[x, g, f], t, peer)

    def sending(x, g, f, act):
        wall = (None, None, at_bottom, at_top)[f]
        straight = None if wall is None else jnp.logical_not(wall)
        if f < 2:
            first = route(f, x)[0]
            rest = jnp.logical_not(first)
            straight = rest if straight is None else jnp.logical_and(straight, rest)
            pl.when(first)(lambda: act(via_copy(x, g, f)))
        if straight is None:
            act(face_copy(x, g, f))
        else:
            pl.when(straight)(lambda: act(face_copy(x, g, f)))

    def pass_on(x, g):
        for f in range(2):

            @pl.when(route(f, x)[1])
            def _(f=f):
                via_copy(x, g, f).wait_recv()
                on_copy(x, g, f).start()

    def raw_copy(v):
        return remote(us.at[v], raw.at[v], raw_s.at[v], raw_r.at[v], beside, e)

    def near_copy(v):
        return remote(us.at[v], near_in.at[v], near_s.at[v], near_r.at[v], opposite, e)

    def far_copy(v):
        return remote(us.at[v], far_in.at[v], far_s.at[v], far_r.at[v], lax.rem(t + 2, 4), e)

    def cross_copy(g, v):
        part = (v, members(g))
        return remote(cross_out.at[part], cross_in.at[part], cross_s.at[g, v], cross_r.at[g, v], opposite, e)

    def edge_copy(g, v):
        part = (v, members(g))
        return remote(edge_out.at[part], edge_in.at[part], edge_s.at[g, v], edge_r.at[g, v], beside, e)

    nodes = pl.ds(0, NODES)
    loads = [
        pltpu.make_async_copy(state_ref.at[n, v, :, 0, :], us.at[v, n, nodes, :], in_s.at[v, n])
        for n in range(4)
        for v in range(NV)
    ]
    loads.append(pltpu.make_async_copy(metric_ref.at[:, 0, :], metric.at[nodes, :], in_s.at[NV, 0]))
    for n in range(4):
        loads.append(pltpu.make_async_copy(pre_ref.at[n, :, 0, :], pre.at[n], in_s.at[NV + 1, n]))
    for load in loads:
        load.start()
    last = pl.ds(NODES, ROWS - NODES)
    tail = pl.ds(ROWS - 8, 8)
    metric[last, :] = jnp.zeros((3, 128), F32)
    for v in range(NV):
        for n in range(4):
            us[v, n, last, :] = jnp.zeros((3, 128), F32)
    ax[:, tail, :] = jnp.zeros((2, 8, 128), F32)

    def clear(n, c):
        for x in range(PASSES + 1):
            for f in range(4):
                stage[x, f, n, tail, :] = jnp.zeros((8, 128), F32)
        return c

    lax.fori_loop(0, 4, clear, 0)

    def extract(source, x, g):
        def one(i, c):
            n = GROUPS[g][0] + i
            for v in range(NV):
                rows = pl.ds(FACE * v, FACE)
                stage[x, 0, n, rows, :] = source[v, n, pl.ds(0, FACE), :]
                stage[x, 1, n, rows, :] = source[v, n, pl.ds(100, FACE), :]
                for k in range(5):
                    stage[x, 2, n, pl.ds(FACE * v + 5 * k, 5), :] = source[v, n, pl.ds(25 * k, 5), :]
                    stage[x, 3, n, pl.ds(FACE * v + 5 * k, 5), :] = source[v, n, pl.ds(25 * k + 20, 5), :]
            return c

        lax.fori_loop(0, GROUPS[g][1], one, 0)

    def send_faces(x, g):
        for f in (0, 1, 2, 3):
            sending(x, g, f, lambda copy: copy.start())

    for load in loads:
        load.wait()

    expected = 7
    for f in range(2):
        expected = expected + jnp.where(route(f, 0)[1], 1, 0)
    pl.semaphore_wait(barrier, expected)

    @pl.when(outer)
    def _():
        order = []
        for v in range(WHOLE, NV):
            order.append(raw_copy(v))
            if v - WHOLE < WHOLE:
                order.append(far_copy(v - WHOLE))
        for v in range(NV - WHOLE, WHOLE):
            order.append(far_copy(v))
        for v in range(WHOLE):
            order.append(raw_copy(v))
        for copy in order:
            copy.start()

    @pl.when(inner)
    def _():
        for v in range(WHOLE):
            near_copy(v).start()

    for g in range(len(GROUPS)):
        extract(us, 0, g)
        send_faces(0, g)

    diagonal = lax.broadcasted_iota(jnp.int32, (FACE, FACE), 0) == lax.broadcasted_iota(
        jnp.int32, (FACE, FACE), 1
    )
    for n in range(4):
        for v in range(NV):
            row = inflow_ref[n, v]
            column = jnp.sum(jnp.where(diagonal, row, 0.0), axis=1, keepdims=True)
            inflow_cols[v, n, pl.ds(0, FACE), :] = jnp.broadcast_to(column, (FACE, 128))

    damping = []
    for d in range(3):
        sums = []
        for v in range(NV):
            total = jnp.abs(jac_ref[v, d, 0])
            for w in range(1, NV):
                total = total + jnp.abs(jac_ref[v, d, w])
            sums.append(total)
        largest = sums[0]
        for v in range(1, NV):
            largest = jnp.maximum(largest, sums[v])
        damping.append(largest)
    var_of = lax.broadcasted_iota(jnp.int32, (1, 128), 1) // FACE
    for v in range(NV):
        rows = pl.ds(ROWS * v, ROWS)
        low_rows = pl.ds(ROWS * (NV + v), ROWS)
        for w in range(NV):
            block = jac_ref[v, 0, w] * pat_ref[0]
            for d in range(1, 3):
                block = block + jac_ref[v, d, w] * pat_ref[d]
            if v == w:
                for d in range(3):
                    block = block + damping[d] * pat_ref[3 + d]
            hi, lo = split(block)
            k_loc[rows, ROWS * w : ROWS * (w + 1)] = hi
            k_loc[low_rows, ROWS * w : ROWS * (w + 1)] = lo
        for f in range(6):
            d, side = f // 2, f % 2
            coef = jnp.zeros((1, 128), F32)
            for w in range(NV):
                value = jac_ref[v, d, w]
                if side == 0:
                    value = value - damping[d] if v == w else value
                else:
                    value = -(value + damping[d]) if v == w else -value
                coef = jnp.where(var_of == w, value, coef)
            hi, lo = split(pat_ref[6 + f] * coef)
            if f < 4:
                k_tr[rows, ROWS * f : ROWS * (f + 1)] = hi
                k_tr[low_rows, ROWS * f : ROWS * (f + 1)] = lo
            else:
                k_loc[rows, ROWS * (f + 1) : ROWS * (f + 2)] = hi
                k_loc[low_rows, ROWS * (f + 1) : ROWS * (f + 2)] = lo

    lane = lax.broadcasted_iota(jnp.int32, (FACE, 128), 1)

    def product(matrix, hi, lo):
        first = jnp.dot(matrix[...], hi, preferred_element_type=F32)
        second = jnp.dot(matrix[pl.ds(0, ROWS * NV), :], lo, preferred_element_type=F32)
        return first[: ROWS * NV] + first[ROWS * NV :] + second

    def local_part(source, g):
        first, count = GROUPS[g]
        for i in range(count):
            n = first + i
            cols = slice(128 * i, 128 * (i + 1))
            for v in range(NV):
                hi, lo = split(source[v, n])
                x_hi[pl.ds(ROWS * v, ROWS), cols] = hi
                x_lo[pl.ds(ROWS * v, ROWS), cols] = lo
                near = source[v, n, pl.ds(0, FACE, stride=5), :]
                far = source[v, n, pl.ds(4, FACE, stride=5), :]
                ax[0, pl.ds(FACE * v, FACE), :] = jnp.where(lane == 127, far, pltpu.roll(near, 127, 1))
                ax[1, pl.ds(FACE * v, FACE), :] = jnp.where(
                    lane == 0, inflow_cols[v, n, pl.ds(0, FACE), :], pltpu.roll(far, 1, 1)
                )
            for f in range(2):
                hi, lo = split(ax[f])
                x_hi[pl.ds(ROWS * (NV + f), ROWS), cols] = hi
                x_lo[pl.ds(ROWS * (NV + f), ROWS), cols] = lo
        used = slice(0, 128 * count)
        total = product(k_loc, x_hi[:, used], x_lo[:, used])
        for i in range(count):
            r[first + i] = total[:, 128 * i : 128 * (i + 1)]

    row = lax.broadcasted_iota(jnp.int32, (ROWS, 128), 0)
    sign = jnp.where(jnp.logical_and(row >= 2 * FACE, row < 3 * FACE), -1.0, 1.0)

    def trace_part(x, g):
        first, count = GROUPS[g]

        def put(f, i, value):
            hi, lo = split(value)
            t_hi[pl.ds(ROWS * f, ROWS), 128 * i : 128 * (i + 1)] = hi
            t_lo[pl.ds(ROWS * f, ROWS), 128 * i : 128 * (i + 1)] = lo

        def arrived(f):
            face_copy(x, g, f).wait_recv()
            for i in range(count):
                put(f, i, faces[x, f, first + i])

        def mirrored(f):
            for i in range(count):
                put(f, i, sign * stage[x, 5 - f, first + i])

        for f, edge in ((2, at_top), (3, at_bottom)):
            pl.when(jnp.logical_not(edge))(functools.partial(arrived, f))
            pl.when(edge)(functools.partial(mirrored, f))
        for f in range(2):
            arrived(f)
        used = slice(0, 128 * count)
        total = product(k_tr, t_hi[:, used], t_lo[:, used])
        for i in range(count):
            r[first + i] = r[first + i] + total[:, 128 * i : 128 * (i + 1)]

    def finish(source, g):
        first, count = GROUPS[g]

        def one(i, c):
            n = first + i // 4
            start = pl.multiple_of(lax.rem(i, 4) * CHUNK, CHUNK)
            rows = pl.ds(start, CHUNK)
            scale = metric[rows, :]
            values = [
                scale * r[n, pl.ds(pl.multiple_of(ROWS * v + start, CHUNK), CHUNK), :] + spec[v, n, rows, :]
                for v in range(NV)
            ]
            for v in range(NV):
                total = pre[n, pl.ds(NV * v, 1), :] * values[0]
                for w in range(1, NV):
                    total = total + pre[n, pl.ds(NV * v + w, 1), :] * values[w]
                u[v, n, rows, :] = source[v, n, rows, :] - total
            return c

        lax.fori_loop(0, 4 * count, one, 0)

    def stores(g, kind):
        buffer, target = ((u, new_ref), (res, res_ref))[kind]
        first, count = GROUPS[g]
        return [
            pltpu.make_async_copy(buffer.at[v, n, nodes, :], target.at[n, v, :, 0, :], out_s.at[kind, v, n])
            for n in range(first, first + count)
            for v in range(NV)
        ]

    def results(g):
        first, count = GROUPS[g]
        for n in range(first, first + count):
            for v in range(NV):
                res[v, n] = metric[...] * r[n, pl.ds(ROWS * v, ROWS), :] + spec[v, n]
        for store in stores(g, 1):
            store.start()

    def weight(offset, n, m):
        return jnp.where(ahead, coupling(4 * offset + n - m), coupling(-4 * offset + n - m)).astype(F32)

    def tiles(body):
        def one(c, carry):
            body(pl.ds(pl.multiple_of(c * 16, 16), 16))
            return carry

        lax.fori_loop(0, 8, one, 0)

    def combine(total, offset, n, values):
        for m in range(4):
            total = total + weight(offset, n, m) * values[m]
        return total

    def own_part(total, n, values):
        for m in range(4):
            if n != m:
                total = total + coupling(n - m) * values[m]
        return total

    def instances(g):
        return range(GROUPS[g][0], GROUPS[g][0] + GROUPS[g][1])

    def send_cross(g, v):
        def body(rows):
            mine = [us[v, m, rows, :] for m in range(4)]
            theirs = [raw[v, m, rows, :] for m in range(4)]
            for n in instances(g):
                for q in range(2):
                    total = combine(jnp.zeros((16, 128), F32), 1 + q, n, mine)
                    cross_out[v, n, q, rows, :] = combine(total, 2 + q, n, theirs)

        tiles(body)
        cross_copy(g, v).start()

    def whole_sums(v):
        raw_copy(v).wait_recv()
        near_copy(v).wait_recv()
        far_copy(v).wait_recv()

        def body(rows):
            mine = [us[v, m, rows, :] for m in range(4)]
            theirs = [raw[v, m, rows, :] for m in range(4)]
            near = [near_in[v, m, rows, :] for m in range(4)]
            far = [far_in[v, m, rows, :] for m in range(4)]
            for n in range(4):
                zero = jnp.zeros((16, 128), F32)
                edge_out[v, n, rows, :] = combine(combine(combine(zero, -1, n, mine), -2, n, near), -3, n, far)
                spec[v, n, rows, :] = combine(
                    combine(combine(own_part(zero, n, mine), 1, n, theirs), -1, n, near), -2, n, far
                )

        tiles(body)
        edge_copy(0, v).start()

    def inner_sums(g, v):
        cross_copy(g, v).wait_recv()

        def body(rows):
            mine = [us[v, m, rows, :] for m in range(4)]
            theirs = [raw[v, m, rows, :] for m in range(4)]
            for n in instances(g):
                edge_out[v, n, rows, :] = combine(cross_in[v, n, 1, rows, :], -1, n, mine)
                spec[v, n, rows, :] = combine(own_part(cross_in[v, n, 0, rows, :], n, mine), 1, n, theirs)

        tiles(body)
        edge_copy(g, v).start()

    def outer_sums(g, v):
        edge_copy(g, v).wait_recv()

        def body(rows):
            mine = [us[v, m, rows, :] for m in range(4)]
            for n in instances(g):
                spec[v, n, rows, :] = own_part(edge_in[v, n, rows, :], n, mine)

        tiles(body)

    def sums(g):
        @pl.when(inner)
        def _():
            for v in range(WHOLE, NV):
                inner_sums(g, v)

        @pl.when(outer)
        def _():
            for v in range(NV):
                outer_sums(g, v)

    def advance(source, x, g):
        finish(source, g)
        extract(u, x + 1, g)
        send_faces(x + 1, g)
        if x == PASSES - 1:
            for store in stores(g, 0):
                store.start()
        local_part(u, g)

    for g in range(len(GROUPS)):
        local_part(us, g)
    for g in range(len(GROUPS)):
        pass_on(0, g)

    @pl.when(inner)
    def _():
        for v in range(WHOLE, NV):
            raw_copy(v).wait_recv()
            send_cross(0, v)
            if v > WHOLE:
                inner_sums(0, v - 1)
        for g in range(1, len(GROUPS)):
            for v in range(WHOLE, NV):
                send_cross(g, v)
        for v in range(WHOLE):
            whole_sums(v)
        inner_sums(0, NV - 1)
        for g in range(1, len(GROUPS)):
            for v in range(WHOLE):
                edge_copy(g, v).start()

    for g in range(len(GROUPS)):
        trace_part(0, g)

    @pl.when(outer)
    def _():
        for v in (*range(WHOLE, NV - 1), *range(WHOLE), NV - 1):
            outer_sums(0, v)

    advance(us, 0, 0)
    for g in range(1, len(GROUPS)):
        sums(g)
        advance(us, 0, g)
        pass_on(1, g - 1)
    pass_on(1, len(GROUPS) - 1)
    for x in range(1, PASSES + 1):
        for g in range(len(GROUPS)):
            trace_part(x, g)
            if x == PASSES:
                results(g)
                continue
            if g > 0:
                pass_on(x + 1, g - 1)
            advance(u, x, g)
        if x < PASSES:
            pass_on(x + 1, len(GROUPS) - 1)

    for g in range(len(GROUPS)):
        for kind in range(2):
            for store in stores(g, kind):
                store.wait()

    for g in range(len(GROUPS)):
        for x in range(PASSES + 1):
            for f in range(4):
                sending(x, g, f, lambda copy: copy.wait_send())
            for f in range(2):

                @pl.when(route(f, x)[1])
                def _(x=x, g=g, f=f):
                    on_copy(x, g, f).wait_send()

    @pl.when(outer)
    def _():
        for v in range(NV):
            raw_copy(v).wait_send()
        for v in range(WHOLE):
            far_copy(v).wait_send()

    @pl.when(inner)
    def _():
        for v in range(WHOLE):
            near_copy(v).wait_send()
        for g in range(len(GROUPS)):
            for v in range(NV):
                if v >= WHOLE:
                    cross_copy(g, v).wait_send()
                edge_copy(g, v).wait_send()


def per_device(state, metric_scale, flux_jacobians, preconditioner, inflow):
    vmem = pl.BlockSpec(memory_space=pltpu.VMEM)
    smem = pl.BlockSpec(memory_space=pltpu.SMEM)
    block = (4, NV, NODES, 1, 128)
    hbm = pl.BlockSpec(memory_space=pl.ANY)
    dma = pltpu.SemaphoreType.DMA
    exchanges = PASSES + 1
    groups = len(GROUPS)
    new_state, residual = pl.pallas_call(
        kernel,
        name="pseudo_step",
        out_shape=(pltpu.VMEM(block, F32), pltpu.VMEM(block, F32)),
        in_specs=[hbm, hbm, smem, hbm, vmem, vmem],
        out_specs=(vmem, vmem),
        scratch_shapes=[
            pltpu.VMEM((NV, 4, ROWS, 128), F32),
            pltpu.VMEM((NV, 4, ROWS, 128), F32),
            pltpu.VMEM((NV, 4, ROWS, 128), F32),
            pltpu.VMEM((NV, 4, ROWS, 128), F32),
            pltpu.VMEM((ROWS, 128), F32),
            pltpu.VMEM((4, NV * NV, 128), F32),
            pltpu.VMEM((NV, 4, 32, 128), F32),
            pltpu.VMEM((2 * NV * ROWS, 7 * ROWS), BF16),
            pltpu.VMEM((2 * NV * ROWS, 4 * ROWS), BF16),
            pltpu.VMEM((7 * ROWS, 256), BF16),
            pltpu.VMEM((7 * ROWS, 256), BF16),
            pltpu.VMEM((4 * ROWS, 256), BF16),
            pltpu.VMEM((4 * ROWS, 256), BF16),
            pltpu.VMEM((4, NV * ROWS, 128), F32),
            pltpu.VMEM((2, ROWS, 128), F32),
            pltpu.VMEM((exchanges, 4, 4, ROWS, 128), F32),
            pltpu.VMEM((exchanges, 4, 4, ROWS, 128), F32),
            pltpu.VMEM((exchanges, 4, 4, ROWS, 128), F32),
            pltpu.VMEM((NV, 4, ROWS, 128), F32),
            pltpu.VMEM((WHOLE, 4, ROWS, 128), F32),
            pltpu.VMEM((WHOLE, 4, ROWS, 128), F32),
            pltpu.VMEM((NV, 4, 2, ROWS, 128), F32),
            pltpu.VMEM((NV, 4, 2, ROWS, 128), F32),
            pltpu.VMEM((NV, 4, ROWS, 128), F32),
            pltpu.VMEM((NV, 4, ROWS, 128), F32),
            dma((exchanges, groups, 4)),
            dma((exchanges, groups, 4)),
            dma((exchanges, groups, 4)),
            dma((exchanges, groups, 4)),
            dma((exchanges, groups, 4)),
            dma((NV,)),
            dma((NV,)),
            dma((WHOLE,)),
            dma((WHOLE,)),
            dma((WHOLE,)),
            dma((WHOLE,)),
            dma((groups, NV)),
            dma((groups, NV)),
            dma((groups, NV)),
            dma((groups, NV)),
            dma((NV + 2, 4)),
            dma((2, NV, 4)),
        ],
        compiler_params=pltpu.CompilerParams(
            collective_id=0, has_side_effects=True, vmem_limit_bytes=60 * 2**20
        ),
    )(
        state.reshape(block),
        metric_scale.reshape(NODES, 1, 128),
        flux_jacobians.transpose(1, 0, 2),
        preconditioner.reshape(4, NV * NV, 1, 128),
        inflow.reshape(4, NV, 1, FACE),
        jnp.asarray(patterns()),
    )
    return new_state.reshape(state.shape), residual.reshape(state.shape)


def solution(mesh):
    in_specs = (
        P("tm", None, "elem", None, None),
        P("elem", None, None),
        P(),
        P("tm", None, None, "elem", None),
        P("tm", None, "elem", None),
    )
    out_specs = (P("tm", None, "elem", None, None), P("tm", None, "elem", None, None))
    return jax.shard_map(
        per_device, mesh=mesh, in_specs=in_specs, out_specs=out_specs, check_vma=False
    )
```

```python
import functools
import math

import jax
import jax.numpy as jnp
import numpy as np
from jax import lax
from jax.experimental import pallas as pl
from jax.experimental.pallas import tpu as pltpu
from jax.sharding import PartitionSpec as P

NI = 16
NV = 5
PR = 8
PASSES = 3
ROWS = 128
NODES = 125
FACE = 25
CHUNK = 32
INSTANCES = 4
WHOLE = 2
MESH = pl.DeviceIdType.MESH
F32 = jnp.float32
BF16 = jnp.bfloat16


def gll_derivative():
    points = np.array([-1.0, -math.sqrt(3.0 / 7.0), 0.0, math.sqrt(3.0 / 7.0), 1.0])
    legendre = (35.0 * points**4 - 30.0 * points**2 + 3.0) / 8.0
    identity = np.eye(5, dtype=bool)
    spacing = np.where(identity, 1.0, points[:, None] - points[None, :])
    matrix = legendre[:, None] / legendre[None, :] / spacing
    corner = np.array([-5.0, 0.0, 0.0, 0.0, 5.0])[None, :]
    return np.where(identity, corner, matrix)


def coupling(offset):
    if offset % NI == 0:
        return 0.0
    angle = math.pi * offset / NI
    return 0.5 * (1.0 - 2.0 * (offset % 2)) * math.cos(angle) / math.sin(angle)


def patterns():
    table = gll_derivative()
    node = np.arange(NODES)
    index = [node // 25, (node // 5) % 5, node % 5]
    out = np.zeros((12, ROWS, ROWS))
    for d in range(3):
        others = [index[o] for o in range(3) if o != d]
        same = np.ones((NODES, NODES), bool)
        for o in others:
            same &= o[:, None] == o[None, :]
        out[d, :NODES, :NODES] = np.where(same, table[index[d][:, None], index[d][None, :]], 0.0)
        high, low = index[d] == 4, index[d] == 0
        out[d, node, node] += np.where(high, -5.0, 0.0) + np.where(low, 5.0, 0.0)
        out[3 + d, node, node] = np.where(high | low, 5.0, 0.0)
        for side, face in enumerate((high, low)):
            dest = node[face]
            for v in range(NV):
                out[6 + 2 * d + side, dest, FACE * v + np.arange(FACE)] = 5.0
    return out.astype(np.float32)


def split(value):
    high = value.astype(BF16)
    low = (value - high.astype(F32)).astype(BF16)
    return high, low


def kernel(
    state_ref, metric_ref, jac_ref, pre_ref, inflow_ref, pat_ref, new_ref, res_ref,
    us, u, spec, res, metric, pre, inflow_cols, k_loc, k_tr, x_hi, x_lo, t_hi, t_lo, r, ax,
    stage, faces, passing, raw, near_in, far_in, cross_out, cross_in, edge_out, edge_in,
    face_s, face_r, via_s, via_r, on_s, raw_s, raw_r, near_s, near_r, far_s, far_r, cross_s, cross_r, edge_s, edge_r, in_s, out_s,
):
    t = lax.axis_index("tm")
    e = lax.axis_index("elem")
    inner = jnp.logical_or(t == 1, t == 2)
    outer = jnp.logical_not(inner)
    ahead = t < 2
    beside = jnp.where(inner, jnp.where(t == 1, 0, 3), jnp.where(t == 0, 1, 2))
    opposite = jnp.where(inner, 3 - t, t)
    at_top = lax.rem(e, PR) == PR // 2 - 1
    at_bottom = lax.rem(e, PR) == PR // 2
    following = lax.rem(e + PR, 64)
    preceding = lax.rem(e + 64 - PR, 64)
    above = lax.rem(e + 1, 64)
    below = lax.rem(e + 63, 64)

    core, x_of, y_of = lax.rem(e, 2), lax.rem(e // 8, 4), lax.rem(e // 2, 4)

    def at(x):
        return jnp.logical_and(x_of == x, core == 1)

    def route(f, x):
        edge, relay, other, distance, row = ((0, 1, 3, -16, 3), (3, 2, 0, 16, 0))[f]
        places = [at(edge), at(relay), at(other)]
        relayed = jnp.logical_or(x < 2, y_of != row)
        places = [jnp.logical_and(place, relayed) for place in places]
        return (*places, distance)

    barrier = pltpu.get_barrier_semaphore()
    for peer in (following, preceding, above, below):
        pl.semaphore_signal(barrier, inc=1, device_id=(t, peer), device_id_type=MESH)
    for step in (1, 3):
        pl.semaphore_signal(barrier, inc=1, device_id=(lax.rem(t + step, 4), e), device_id_type=MESH)

    for f in range(2):
        _, _, last_device, distance = route(f, 0)

        @pl.when(last_device)
        def _(distance=distance):
            relay = lax.rem(e + 64 - distance, 64)
            pl.semaphore_signal(barrier, inc=1, device_id=(t, relay), device_id_type=MESH)

    def remote(source, target, send, recv, peer_t, peer_e):
        return pltpu.make_async_remote_copy(
            src_ref=source, dst_ref=target, send_sem=send, recv_sem=recv,
            device_id=(peer_t, peer_e), device_id_type=MESH,
        )

    def face_copy(x, g, f):
        peer = (preceding, following, below, above)[f]
        part = (x, f, g)
        return remote(stage.at[part], faces.at[part], face_s.at[x, g, f], face_r.at[x, g, f], t, peer)

    def via_copy(x, g, f):
        peer = (following, preceding)[f % 2]
        part = (x, f, g)
        return remote(stage.at[part], passing.at[part], via_s.at[x, g, f], via_r.at[x, g, f], t, peer)

    def on_copy(x, g, f):
        part = (x, f, g)
        peer = lax.rem(e + 64 + route(f, x)[3], 64)
        return remote(passing.at[part], faces.at[part], on_s.at[x, g, f], face_r.at[x, g, f], t, peer)

    def sending(x, g, f, act):
        wall = (None, None, at_bottom, at_top)[f]
        straight = None if wall is None else jnp.logical_not(wall)
        if f < 2:
            first = route(f, x)[0]
            rest = jnp.logical_not(first)
            straight = rest if straight is None else jnp.logical_and(straight, rest)
            pl.when(first)(lambda: act(via_copy(x, g, f)))
        if straight is None:
            act(face_copy(x, g, f))
        else:
            pl.when(straight)(lambda: act(face_copy(x, g, f)))

    def pass_on(x, g):
        for f in range(2):

            @pl.when(route(f, x)[1])
            def _(f=f):
                via_copy(x, g, f).wait_recv()
                on_copy(x, g, f).start()

    def raw_copy(v):
        return remote(us.at[v], raw.at[v], raw_s.at[v], raw_r.at[v], beside, e)

    def near_copy(v):
        return remote(us.at[v], near_in.at[v], near_s.at[v], near_r.at[v], opposite, e)

    def far_copy(v):
        return remote(raw.at[v], far_in.at[v], far_s.at[v], far_r.at[v], opposite, e)

    def cross_copy(g, v):
        part = (v, g)
        return remote(cross_out.at[part], cross_in.at[part], cross_s.at[g, v], cross_r.at[g, v], opposite, e)

    def edge_copy(g, v):
        part = (v, g)
        return remote(edge_out.at[part], edge_in.at[part], edge_s.at[g, v], edge_r.at[g, v], beside, e)

    nodes = pl.ds(0, NODES)
    loads = [
        pltpu.make_async_copy(state_ref.at[n, v, :, 0, :], us.at[v, n, nodes, :], in_s.at[v, n])
        for n in range(4)
        for v in range(NV)
    ]
    loads.append(pltpu.make_async_copy(metric_ref.at[:, 0, :], metric.at[nodes, :], in_s.at[NV, 0]))
    for n in range(4):
        loads.append(pltpu.make_async_copy(pre_ref.at[n, :, 0, :], pre.at[n], in_s.at[NV + 1, n]))
    for load in loads:
        load.start()
    last = pl.ds(NODES, ROWS - NODES)
    tail = pl.ds(ROWS - 8, 8)
    metric[last, :] = jnp.zeros((3, 128), F32)
    for v in range(NV):
        for n in range(4):
            us[v, n, last, :] = jnp.zeros((3, 128), F32)
    ax[:, tail, :] = jnp.zeros((2, 8, 128), F32)

    def clear(n, c):
        for x in range(PASSES + 1):
            for f in range(4):
                stage[x, f, n, tail, :] = jnp.zeros((8, 128), F32)
        return c

    lax.fori_loop(0, 4, clear, 0)

    def extract(source, x, g):
        for v in range(NV):
            rows = pl.ds(FACE * v, FACE)
            stage[x, 0, g, rows, :] = source[v, g, pl.ds(0, FACE), :]
            stage[x, 1, g, rows, :] = source[v, g, pl.ds(100, FACE), :]
            for k in range(5):
                stage[x, 2, g, pl.ds(FACE * v + 5 * k, 5), :] = source[v, g, pl.ds(25 * k, 5), :]
                stage[x, 3, g, pl.ds(FACE * v + 5 * k, 5), :] = source[v, g, pl.ds(25 * k + 20, 5), :]

    def send_faces(x, g):
        for f in (0, 1, 2, 3):
            sending(x, g, f, lambda copy: copy.start())

    for load in loads:
        load.wait()

    expected = 6
    for f in range(2):
        expected = expected + jnp.where(route(f, 0)[1], 1, 0)
    pl.semaphore_wait(barrier, expected)

    @pl.when(outer)
    def _():
        for v in range(NV):
            raw_copy(v).start()

    @pl.when(inner)
    def _():
        for v in range(WHOLE):
            near_copy(v).start()

    def each(body):
        def one(g, c):
            body(g)
            return c

        lax.fori_loop(0, INSTANCES, one, 0)

    def begin(g):
        extract(us, 0, g)
        send_faces(0, g)

    each(begin)

    diagonal = lax.broadcasted_iota(jnp.int32, (FACE, FACE), 0) == lax.broadcasted_iota(
        jnp.int32, (FACE, FACE), 1
    )
    for n in range(4):
        for v in range(NV):
            row = inflow_ref[n, v]
            column = jnp.sum(jnp.where(diagonal, row, 0.0), axis=1, keepdims=True)
            inflow_cols[v, n, pl.ds(0, FACE), :] = jnp.broadcast_to(column, (FACE, 128))

    damping = []
    for d in range(3):
        sums = []
        for v in range(NV):
            total = jnp.abs(jac_ref[v, d, 0])
            for w in range(1, NV):
                total = total + jnp.abs(jac_ref[v, d, w])
            sums.append(total)
        largest = sums[0]
        for v in range(1, NV):
            largest = jnp.maximum(largest, sums[v])
        damping.append(largest)
    var_of = lax.broadcasted_iota(jnp.int32, (1, 128), 1) // FACE
    for v in range(NV):
        rows = pl.ds(ROWS * v, ROWS)
        low_rows = pl.ds(ROWS * (NV + v), ROWS)
        for w in range(NV):
            block = jac_ref[v, 0, w] * pat_ref[0]
            for d in range(1, 3):
                block = block + jac_ref[v, d, w] * pat_ref[d]
            if v == w:
                for d in range(3):
                    block = block + damping[d] * pat_ref[3 + d]
            hi, lo = split(block)
            k_loc[rows, ROWS * w : ROWS * (w + 1)] = hi
            k_loc[low_rows, ROWS * w : ROWS * (w + 1)] = lo
        for f in range(6):
            d, side = f // 2, f % 2
            coef = jnp.zeros((1, 128), F32)
            for w in range(NV):
                value = jac_ref[v, d, w]
                if side == 0:
                    value = value - damping[d] if v == w else value
                else:
                    value = -(value + damping[d]) if v == w else -value
                coef = jnp.where(var_of == w, value, coef)
            hi, lo = split(pat_ref[6 + f] * coef)
            if f < 4:
                k_tr[rows, ROWS * f : ROWS * (f + 1)] = hi
                k_tr[low_rows, ROWS * f : ROWS * (f + 1)] = lo
            else:
                k_loc[rows, ROWS * (f + 1) : ROWS * (f + 2)] = hi
                k_loc[low_rows, ROWS * (f + 1) : ROWS * (f + 2)] = lo

    lane = lax.broadcasted_iota(jnp.int32, (FACE, 128), 1)

    def product(matrix, hi, lo):
        first = jnp.dot(matrix[...], hi, preferred_element_type=F32)
        second = jnp.dot(matrix[pl.ds(0, ROWS * NV), :], lo, preferred_element_type=F32)
        return first[: ROWS * NV] + first[ROWS * NV :] + second

    def local_part(source, g):
        for v in range(NV):
            hi, lo = split(source[v, g])
            x_hi[pl.ds(ROWS * v, ROWS), :] = hi
            x_lo[pl.ds(ROWS * v, ROWS), :] = lo
            near = source[v, g, pl.ds(0, FACE, stride=5), :]
            far = source[v, g, pl.ds(4, FACE, stride=5), :]
            ax[0, pl.ds(FACE * v, FACE), :] = jnp.where(lane == 127, far, pltpu.roll(near, 127, 1))
            ax[1, pl.ds(FACE * v, FACE), :] = jnp.where(
                lane == 0, inflow_cols[v, g, pl.ds(0, FACE), :], pltpu.roll(far, 1, 1)
            )
        for f in range(2):
            hi, lo = split(ax[f])
            x_hi[pl.ds(ROWS * (NV + f), ROWS), :] = hi
            x_lo[pl.ds(ROWS * (NV + f), ROWS), :] = lo
        r[g] = product(k_loc, x_hi[...], x_lo[...])

    row = lax.broadcasted_iota(jnp.int32, (ROWS, 128), 0)
    sign = jnp.where(jnp.logical_and(row >= 2 * FACE, row < 3 * FACE), -1.0, 1.0)

    def trace_part(x, g):
        def put(f, value):
            hi, lo = split(value)
            t_hi[pl.ds(ROWS * f, ROWS), :] = hi
            t_lo[pl.ds(ROWS * f, ROWS), :] = lo

        def arrived(f):
            face_copy(x, g, f).wait_recv()
            put(f, faces[x, f, g])

        def mirrored(f):
            put(f, sign * stage[x, 5 - f, g])

        for f, edge in ((2, at_top), (3, at_bottom)):
            pl.when(jnp.logical_not(edge))(functools.partial(arrived, f))
            pl.when(edge)(functools.partial(mirrored, f))
        for f in range(2):
            arrived(f)
        r[g] = r[g] + product(k_tr, t_hi[...], t_lo[...])

    def finish(source, g):
        n = g

        def one(i, c):
            start = pl.multiple_of(i * CHUNK, CHUNK)
            rows = pl.ds(start, CHUNK)
            scale = metric[rows, :]
            values = [
                scale * r[n, pl.ds(pl.multiple_of(ROWS * v + start, CHUNK), CHUNK), :] + spec[v, n, rows, :]
                for v in range(NV)
            ]
            for v in range(NV):
                total = pre[n, pl.ds(NV * v, 1), :] * values[0]
                for w in range(1, NV):
                    total = total + pre[n, pl.ds(NV * v + w, 1), :] * values[w]
                u[v, n, rows, :] = source[v, n, rows, :] - total
            return c

        lax.fori_loop(0, ROWS // CHUNK, one, 0)

    def stores(g, kind):
        buffer, target = ((u, new_ref), (res, res_ref))[kind]
        return [
            pltpu.make_async_copy(buffer.at[v, g, nodes, :], target.at[g, v, :, 0, :], out_s.at[kind, v, g])
            for v in range(NV)
        ]

    def results(g):
        for v in range(NV):
            res[v, g] = metric[...] * r[g, pl.ds(ROWS * v, ROWS), :] + spec[v, g]
        for store in stores(g, 1):
            store.start()

    def weight(offset, n, m):
        return jnp.where(ahead, coupling(4 * offset + n - m), coupling(-4 * offset + n - m)).astype(F32)

    def tiles(body):
        def one(c, carry):
            body(pl.ds(pl.multiple_of(c * 16, 16), 16))
            return carry

        lax.fori_loop(0, 8, one, 0)

    def combine(total, offset, n, values):
        for m in range(4):
            total = total + weight(offset, n, m) * values[m]
        return total

    def own_part(total, n, values):
        for m in range(4):
            if n != m:
                total = total + coupling(n - m) * values[m]
        return total

    def send_cross(g, v):
        def body(rows):
            mine = [us[v, m, rows, :] for m in range(4)]
            theirs = [raw[v, m, rows, :] for m in range(4)]
            for n in (g,):
                for q in range(2):
                    total = combine(jnp.zeros((16, 128), F32), 1 + q, n, mine)
                    cross_out[v, n, q, rows, :] = combine(total, 2 + q, n, theirs)

        tiles(body)
        cross_copy(g, v).start()

    def whole_sums(v):
        near_copy(v).wait_recv()
        far_copy(v).wait_recv()

        def body(rows):
            mine = [us[v, m, rows, :] for m in range(4)]
            theirs = [raw[v, m, rows, :] for m in range(4)]
            near = [near_in[v, m, rows, :] for m in range(4)]
            far = [far_in[v, m, rows, :] for m in range(4)]
            for n in range(4):
                zero = jnp.zeros((16, 128), F32)
                edge_out[v, n, rows, :] = combine(combine(combine(zero, -1, n, mine), -2, n, near), -3, n, far)
                spec[v, n, rows, :] = combine(
                    combine(combine(own_part(zero, n, mine), 1, n, theirs), -1, n, near), -2, n, far
                )

        tiles(body)
        for g in range(2):
            edge_copy(g, v).start()

    def inner_sums(g, v):
        cross_copy(g, v).wait_recv()

        def body(rows):
            mine = [us[v, m, rows, :] for m in range(4)]
            theirs = [raw[v, m, rows, :] for m in range(4)]
            for n in (g,):
                edge_out[v, n, rows, :] = combine(cross_in[v, n, 1, rows, :], -1, n, mine)
                spec[v, n, rows, :] = combine(own_part(cross_in[v, n, 0, rows, :], n, mine), 1, n, theirs)

        tiles(body)
        edge_copy(g, v).start()

    def outer_sums(g, v):
        edge_copy(g, v).wait_recv()

        def body(rows):
            mine = [us[v, m, rows, :] for m in range(4)]
            for n in (g,):
                spec[v, n, rows, :] = own_part(edge_in[v, n, rows, :], n, mine)

        tiles(body)

    def sums(g):
        @pl.when(inner)
        def _():
            for v in range(WHOLE if g >= 2 else NV - 1, NV):
                inner_sums(g, v)

        @pl.when(outer)
        def _():
            for v in range(NV):
                outer_sums(g, v)

    def advance(source, x, g):
        finish(source, g)
        extract(u, x + 1, g)
        send_faces(x + 1, g)

        @pl.when(x == PASSES - 1)
        def _():
            for store in stores(g, 0):
                store.start()

        local_part(u, g)

    each(lambda g: local_part(us, g))
    each(lambda g: pass_on(0, g))

    @pl.when(inner)
    def _():
        for v in range(WHOLE):
            raw_copy(v).wait_recv()
            far_copy(v).start()
        for v in range(WHOLE, NV):
            raw_copy(v).wait_recv()
            for g in range(2):
                send_cross(g, v)
            if v - WHOLE < WHOLE:
                whole_sums(v - WHOLE)
        for g in range(2, INSTANCES):
            for v in range(WHOLE, NV):
                send_cross(g, v)
        for v in range(WHOLE, NV - 1):
            for g in range(2):
                inner_sums(g, v)

    each(lambda g: trace_part(0, g))

    for g in range(INSTANCES):
        sums(g)
        if g == 1:

            @pl.when(inner)
            def _():
                for n in range(2, INSTANCES):
                    for v in range(WHOLE):
                        edge_copy(n, v).start()

        advance(us, 0, g)
        if g > 0:
            pass_on(1, g - 1)
    pass_on(1, INSTANCES - 1)

    def middle(i, c):
        x, g = 1 + i // INSTANCES, lax.rem(i, INSTANCES)
        trace_part(x, g)

        @pl.when(g > 0)
        def _():
            pass_on(x + 1, g - 1)

        advance(u, x, g)

        @pl.when(g == INSTANCES - 1)
        def _():
            pass_on(x + 1, g)

        return c

    lax.fori_loop(0, (PASSES - 1) * INSTANCES, middle, 0)

    def end(g):
        trace_part(PASSES, g)
        results(g)

    each(end)

    def drain(g):
        for kind in range(2):
            for store in stores(g, kind):
                store.wait()
        for x in range(PASSES + 1):
            for f in range(4):
                sending(x, g, f, lambda copy: copy.wait_send())
            for f in range(2):

                @pl.when(route(f, x)[1])
                def _(x=x, f=f):
                    on_copy(x, g, f).wait_send()

    each(drain)

    @pl.when(outer)
    def _():
        for v in range(NV):
            raw_copy(v).wait_send()

    @pl.when(inner)
    def _():
        for v in range(WHOLE):
            near_copy(v).wait_send()
            far_copy(v).wait_send()
        for g in range(INSTANCES):
            for v in range(NV):
                if v >= WHOLE:
                    cross_copy(g, v).wait_send()
                edge_copy(g, v).wait_send()


def per_device(state, metric_scale, flux_jacobians, preconditioner, inflow):
    vmem = pl.BlockSpec(memory_space=pltpu.VMEM)
    smem = pl.BlockSpec(memory_space=pltpu.SMEM)
    block = (4, NV, NODES, 1, 128)
    hbm = pl.BlockSpec(memory_space=pl.ANY)
    dma = pltpu.SemaphoreType.DMA
    exchanges = PASSES + 1
    groups = INSTANCES
    new_state, residual = pl.pallas_call(
        kernel,
        name="pseudo_step",
        out_shape=(pltpu.VMEM(block, F32), pltpu.VMEM(block, F32)),
        in_specs=[hbm, hbm, smem, hbm, vmem, vmem],
        out_specs=(vmem, vmem),
        scratch_shapes=[
            pltpu.VMEM((NV, 4, ROWS, 128), F32),
            pltpu.VMEM((NV, 4, ROWS, 128), F32),
            pltpu.VMEM((NV, 4, ROWS, 128), F32),
            pltpu.VMEM((NV, 4, ROWS, 128), F32),
            pltpu.VMEM((ROWS, 128), F32),
            pltpu.VMEM((4, NV * NV, 128), F32),
            pltpu.VMEM((NV, 4, 32, 128), F32),
            pltpu.VMEM((2 * NV * ROWS, 7 * ROWS), BF16),
            pltpu.VMEM((2 * NV * ROWS, 4 * ROWS), BF16),
            pltpu.VMEM((7 * ROWS, 128), BF16),
            pltpu.VMEM((7 * ROWS, 128), BF16),
            pltpu.VMEM((4 * ROWS, 128), BF16),
            pltpu.VMEM((4 * ROWS, 128), BF16),
            pltpu.VMEM((4, NV * ROWS, 128), F32),
            pltpu.VMEM((2, ROWS, 128), F32),
            pltpu.VMEM((exchanges, 4, 4, ROWS, 128), F32),
            pltpu.VMEM((exchanges, 4, 4, ROWS, 128), F32),
            pltpu.VMEM((exchanges, 4, 4, ROWS, 128), F32),
            pltpu.VMEM((NV, 4, ROWS, 128), F32),
            pltpu.VMEM((WHOLE, 4, ROWS, 128), F32),
            pltpu.VMEM((WHOLE, 4, ROWS, 128), F32),
            pltpu.VMEM((NV, 4, 2, ROWS, 128), F32),
            pltpu.VMEM((NV, 4, 2, ROWS, 128), F32),
            pltpu.VMEM((NV, 4, ROWS, 128), F32),
            pltpu.VMEM((NV, 4, ROWS, 128), F32),
            dma((exchanges, groups, 4)),
            dma((exchanges, groups, 4)),
            dma((exchanges, groups, 4)),
            dma((exchanges, groups, 4)),
            dma((exchanges, groups, 4)),
            dma((NV,)),
            dma((NV,)),
            dma((WHOLE,)),
            dma((WHOLE,)),
            dma((WHOLE,)),
            dma((WHOLE,)),
            dma((groups, NV)),
            dma((groups, NV)),
            dma((groups, NV)),
            dma((groups, NV)),
            dma((NV + 2, 4)),
            dma((2, NV, 4)),
        ],
        compiler_params=pltpu.CompilerParams(
            collective_id=0, has_side_effects=True, vmem_limit_bytes=60 * 2**20
        ),
    )(
        state.reshape(block),
        metric_scale.reshape(NODES, 1, 128),
        flux_jacobians.transpose(1, 0, 2),
        preconditioner.reshape(4, NV * NV, 1, 128),
        inflow.reshape(4, NV, 1, FACE),
        jnp.asarray(patterns()),
    )
    return new_state.reshape(state.shape), residual.reshape(state.shape)


def solution(mesh):
    in_specs = (
        P("tm", None, "elem", None, None),
        P("elem", None, None),
        P(),
        P("tm", None, None, "elem", None),
        P("tm", None, "elem", None),
    )
    out_specs = (P("tm", None, "elem", None, None), P("tm", None, "elem", None, None))
    return jax.shard_map(
        per_device, mesh=mesh, in_specs=in_specs, out_specs=out_specs, check_vma=False
    )
```

```python
import functools
import math

import jax
import jax.numpy as jnp
import numpy as np
from jax import lax
from jax.experimental import pallas as pl
from jax.experimental.pallas import tpu as pltpu
from jax.sharding import PartitionSpec as P

NI = 16
NV = 5
PR = 8
PASSES = 3
ROWS = 128
NODES = 125
FACE = 25
CHUNK = 32
INSTANCES = 4
WHOLE = 2
MESH = pl.DeviceIdType.MESH
F32 = jnp.float32
BF16 = jnp.bfloat16


def gll_derivative():
    points = np.array([-1.0, -math.sqrt(3.0 / 7.0), 0.0, math.sqrt(3.0 / 7.0), 1.0])
    legendre = (35.0 * points**4 - 30.0 * points**2 + 3.0) / 8.0
    identity = np.eye(5, dtype=bool)
    spacing = np.where(identity, 1.0, points[:, None] - points[None, :])
    matrix = legendre[:, None] / legendre[None, :] / spacing
    corner = np.array([-5.0, 0.0, 0.0, 0.0, 5.0])[None, :]
    return np.where(identity, corner, matrix)


def coupling(offset):
    if offset % NI == 0:
        return 0.0
    angle = math.pi * offset / NI
    return 0.5 * (1.0 - 2.0 * (offset % 2)) * math.cos(angle) / math.sin(angle)


def patterns():
    table = gll_derivative()
    node = np.arange(NODES)
    index = [node // 25, (node // 5) % 5, node % 5]
    out = np.zeros((12, ROWS, ROWS))
    for d in range(3):
        others = [index[o] for o in range(3) if o != d]
        same = np.ones((NODES, NODES), bool)
        for o in others:
            same &= o[:, None] == o[None, :]
        out[d, :NODES, :NODES] = np.where(same, table[index[d][:, None], index[d][None, :]], 0.0)
        high, low = index[d] == 4, index[d] == 0
        out[d, node, node] += np.where(high, -5.0, 0.0) + np.where(low, 5.0, 0.0)
        out[3 + d, node, node] = np.where(high | low, 5.0, 0.0)
        for side, face in enumerate((high, low)):
            dest = node[face]
            for v in range(NV):
                out[6 + 2 * d + side, dest, FACE * v + np.arange(FACE)] = 5.0
    return out.astype(np.float32)


def split(value):
    high = value.astype(BF16)
    low = (value - high.astype(F32)).astype(BF16)
    return high, low


def kernel(
    state_ref, metric_ref, jac_ref, pre_ref, inflow_ref, pat_ref, new_ref, res_ref,
    us, u, spec, res, metric, pre, inflow_cols, k_loc, k_tr, x_hi, x_lo, t_hi, t_lo, r, ax,
    stage, faces, passing, raw, near_in, far_in, cross_out, cross_in, edge_out, edge_in,
    face_s, face_r, via_s, via_r, on_s, raw_s, raw_r, near_s, near_r, far_s, far_r, cross_s, cross_r, edge_s, edge_r, in_s, out_s,
):
    t = lax.axis_index("tm")
    e = lax.axis_index("elem")
    inner = jnp.logical_or(t == 1, t == 2)
    outer = jnp.logical_not(inner)
    ahead = t < 2
    beside = jnp.where(inner, jnp.where(t == 1, 0, 3), jnp.where(t == 0, 1, 2))
    opposite = jnp.where(inner, 3 - t, t)
    at_top = lax.rem(e, PR) == PR // 2 - 1
    at_bottom = lax.rem(e, PR) == PR // 2
    following = lax.rem(e + PR, 64)
    preceding = lax.rem(e + 64 - PR, 64)
    above = lax.rem(e + 1, 64)
    below = lax.rem(e + 63, 64)

    core, x_of, y_of = lax.rem(e, 2), lax.rem(e // 8, 4), lax.rem(e // 2, 4)

    def at(x):
        return jnp.logical_and(x_of == x, core == 1)

    def route(f, x):
        edge, relay, other, distance, row = ((0, 1, 3, -16, 3), (3, 2, 0, 16, 0))[f]
        places = [at(edge), at(relay), at(other)]
        relayed = jnp.logical_or(x < 2, y_of != row)
        places = [jnp.logical_and(place, relayed) for place in places]
        return (*places, distance)

    barrier = pltpu.get_barrier_semaphore()
    for peer in (following, preceding, above, below):
        pl.semaphore_signal(barrier, inc=1, device_id=(t, peer), device_id_type=MESH)
    for step in (1, 3):
        pl.semaphore_signal(barrier, inc=1, device_id=(lax.rem(t + step, 4), e), device_id_type=MESH)

    for f in range(2):
        _, _, last_device, distance = route(f, 0)

        @pl.when(last_device)
        def _(distance=distance):
            relay = lax.rem(e + 64 - distance, 64)
            pl.semaphore_signal(barrier, inc=1, device_id=(t, relay), device_id_type=MESH)

    def remote(source, target, send, recv, peer_t, peer_e):
        return pltpu.make_async_remote_copy(
            src_ref=source, dst_ref=target, send_sem=send, recv_sem=recv,
            device_id=(peer_t, peer_e), device_id_type=MESH,
        )

    def face_copy(x, g, f):
        peer = (preceding, following, below, above)[f]
        part = (x, f, g)
        return remote(stage.at[part], faces.at[part], face_s.at[x, g, f], face_r.at[x, g, f], t, peer)

    def via_copy(x, g, f):
        peer = (following, preceding)[f % 2]
        part = (x, f, g)
        return remote(stage.at[part], passing.at[part], via_s.at[x, g, f], via_r.at[x, g, f], t, peer)

    def on_copy(x, g, f):
        part = (x, f, g)
        peer = lax.rem(e + 64 + route(f, x)[3], 64)
        return remote(passing.at[part], faces.at[part], on_s.at[x, g, f], face_r.at[x, g, f], t, peer)

    def sending(x, g, f, act):
        wall = (None, None, at_bottom, at_top)[f]
        straight = None if wall is None else jnp.logical_not(wall)
        if f < 2:
            first = route(f, x)[0]
            rest = jnp.logical_not(first)
            straight = rest if straight is None else jnp.logical_and(straight, rest)
            pl.when(first)(lambda: act(via_copy(x, g, f)))
        if straight is None:
            act(face_copy(x, g, f))
        else:
            pl.when(straight)(lambda: act(face_copy(x, g, f)))

    def pass_on(x, g):
        for f in range(2):

            @pl.when(route(f, x)[1])
            def _(f=f):
                via_copy(x, g, f).wait_recv()
                on_copy(x, g, f).start()

    def raw_copy(v):
        return remote(us.at[v], raw.at[v], raw_s.at[v], raw_r.at[v], beside, e)

    def near_copy(v):
        return remote(us.at[v], near_in.at[v], near_s.at[v], near_r.at[v], opposite, e)

    def far_copy(v):
        return remote(raw.at[v], far_in.at[v], far_s.at[v], far_r.at[v], opposite, e)

    def cross_copy(g, v):
        part = (v, g)
        return remote(cross_out.at[part], cross_in.at[part], cross_s.at[g, v], cross_r.at[g, v], opposite, e)

    def edge_copy(g, v):
        part = (v, g)
        return remote(edge_out.at[part], edge_in.at[part], edge_s.at[g, v], edge_r.at[g, v], beside, e)

    nodes = pl.ds(0, NODES)
    loads = [
        pltpu.make_async_copy(state_ref.at[n, v, :, 0, :], us.at[v, n, nodes, :], in_s.at[v, n])
        for n in range(4)
        for v in range(NV)
    ]
    loads.append(pltpu.make_async_copy(metric_ref.at[:, 0, :], metric.at[nodes, :], in_s.at[NV, 0]))
    for n in range(4):
        loads.append(pltpu.make_async_copy(pre_ref.at[n, :, 0, :], pre.at[n], in_s.at[NV + 1, n]))
    for load in loads:
        load.start()
    last = pl.ds(NODES, ROWS - NODES)
    tail = pl.ds(ROWS - 8, 8)
    metric[last, :] = jnp.zeros((3, 128), F32)
    for v in range(NV):
        for n in range(4):
            us[v, n, last, :] = jnp.zeros((3, 128), F32)
    ax[:, tail, :] = jnp.zeros((2, 8, 128), F32)

    def clear(n, c):
        for x in range(PASSES + 1):
            for f in range(4):
                stage[x, f, n, tail, :] = jnp.zeros((8, 128), F32)
        return c

    lax.fori_loop(0, 4, clear, 0)

    def extract(source, x, g):
        for v in range(NV):
            rows = pl.ds(FACE * v, FACE)
            stage[x, 0, g, rows, :] = source[v, g, pl.ds(0, FACE), :]
            stage[x, 1, g, rows, :] = source[v, g, pl.ds(100, FACE), :]
            for k in range(5):
                stage[x, 2, g, pl.ds(FACE * v + 5 * k, 5), :] = source[v, g, pl.ds(25 * k, 5), :]
                stage[x, 3, g, pl.ds(FACE * v + 5 * k, 5), :] = source[v, g, pl.ds(25 * k + 20, 5), :]

    def send_faces(x, g):
        for f in (2, 3, 0, 1):
            sending(x, g, f, lambda copy: copy.start())

    for load in loads:
        load.wait()

    expected = 6
    for f in range(2):
        expected = expected + jnp.where(route(f, 0)[1], 1, 0)
    pl.semaphore_wait(barrier, expected)

    @pl.when(outer)
    def _():
        for v in range(NV):
            raw_copy(v).start()

    @pl.when(inner)
    def _():
        for v in range(WHOLE):
            near_copy(v).start()

    def each(body):
        def one(g, c):
            body(g)
            return c

        lax.fori_loop(0, INSTANCES, one, 0)

    def begin(g):
        extract(us, 0, g)
        send_faces(0, g)

    each(begin)

    diagonal = lax.broadcasted_iota(jnp.int32, (FACE, FACE), 0) == lax.broadcasted_iota(
        jnp.int32, (FACE, FACE), 1
    )
    for n in range(4):
        for v in range(NV):
            row = inflow_ref[n, v]
            column = jnp.sum(jnp.where(diagonal, row, 0.0), axis=1, keepdims=True)
            inflow_cols[v, n, pl.ds(0, FACE), :] = jnp.broadcast_to(column, (FACE, 128))

    damping = []
    for d in range(3):
        sums = []
        for v in range(NV):
            total = jnp.abs(jac_ref[v, d, 0])
            for w in range(1, NV):
                total = total + jnp.abs(jac_ref[v, d, w])
            sums.append(total)
        largest = sums[0]
        for v in range(1, NV):
            largest = jnp.maximum(largest, sums[v])
        damping.append(largest)
    var_of = lax.broadcasted_iota(jnp.int32, (1, 128), 1) // FACE
    for v in range(NV):
        rows = pl.ds(ROWS * v, ROWS)
        low_rows = pl.ds(ROWS * (NV + v), ROWS)
        for w in range(NV):
            block = jac_ref[v, 0, w] * pat_ref[0]
            for d in range(1, 3):
                block = block + jac_ref[v, d, w] * pat_ref[d]
            if v == w:
                for d in range(3):
                    block = block + damping[d] * pat_ref[3 + d]
            hi, lo = split(block)
            k_loc[rows, ROWS * w : ROWS * (w + 1)] = hi
            k_loc[low_rows, ROWS * w : ROWS * (w + 1)] = lo
        for f in range(6):
            d, side = f // 2, f % 2
            coef = jnp.zeros((1, 128), F32)
            for w in range(NV):
                value = jac_ref[v, d, w]
                if side == 0:
                    value = value - damping[d] if v == w else value
                else:
                    value = -(value + damping[d]) if v == w else -value
                coef = jnp.where(var_of == w, value, coef)
            hi, lo = split(pat_ref[6 + f] * coef)
            if f < 4:
                k_tr[rows, ROWS * f : ROWS * (f + 1)] = hi
                k_tr[low_rows, ROWS * f : ROWS * (f + 1)] = lo
            else:
                k_loc[rows, ROWS * (f + 1) : ROWS * (f + 2)] = hi
                k_loc[low_rows, ROWS * (f + 1) : ROWS * (f + 2)] = lo

    lane = lax.broadcasted_iota(jnp.int32, (FACE, 128), 1)

    def product(matrix, hi, lo):
        first = jnp.dot(matrix[...], hi, preferred_element_type=F32)
        second = jnp.dot(matrix[pl.ds(0, ROWS * NV), :], lo, preferred_element_type=F32)
        return first[: ROWS * NV] + first[ROWS * NV :] + second

    def local_part(source, g):
        for v in range(NV):
            hi, lo = split(source[v, g])
            x_hi[pl.ds(ROWS * v, ROWS), :] = hi
            x_lo[pl.ds(ROWS * v, ROWS), :] = lo
            near = source[v, g, pl.ds(0, FACE, stride=5), :]
            far = source[v, g, pl.ds(4, FACE, stride=5), :]
            ax[0, pl.ds(FACE * v, FACE), :] = jnp.where(lane == 127, far, pltpu.roll(near, 127, 1))
            ax[1, pl.ds(FACE * v, FACE), :] = jnp.where(
                lane == 0, inflow_cols[v, g, pl.ds(0, FACE), :], pltpu.roll(far, 1, 1)
            )
        for f in range(2):
            hi, lo = split(ax[f])
            x_hi[pl.ds(ROWS * (NV + f), ROWS), :] = hi
            x_lo[pl.ds(ROWS * (NV + f), ROWS), :] = lo
        r[g] = product(k_loc, x_hi[...], x_lo[...])

    row = lax.broadcasted_iota(jnp.int32, (ROWS, 128), 0)
    sign = jnp.where(jnp.logical_and(row >= 2 * FACE, row < 3 * FACE), -1.0, 1.0)

    def trace_part(x, g):
        def put(f, value):
            hi, lo = split(value)
            t_hi[pl.ds(ROWS * f, ROWS), :] = hi
            t_lo[pl.ds(ROWS * f, ROWS), :] = lo

        def arrived(f):
            face_copy(x, g, f).wait_recv()
            put(f, faces[x, f, g])

        def mirrored(f):
            put(f, sign * stage[x, 5 - f, g])

        for f, edge in ((2, at_top), (3, at_bottom)):
            pl.when(jnp.logical_not(edge))(functools.partial(arrived, f))
            pl.when(edge)(functools.partial(mirrored, f))
        for f in range(2):
            arrived(f)
        r[g] = r[g] + product(k_tr, t_hi[...], t_lo[...])

    def finish(source, g):
        n = g

        def one(i, c):
            start = pl.multiple_of(i * CHUNK, CHUNK)
            rows = pl.ds(start, CHUNK)
            scale = metric[rows, :]
            values = [
                scale * r[n, pl.ds(pl.multiple_of(ROWS * v + start, CHUNK), CHUNK), :] + spec[v, n, rows, :]
                for v in range(NV)
            ]
            for v in range(NV):
                total = pre[n, pl.ds(NV * v, 1), :] * values[0]
                for w in range(1, NV):
                    total = total + pre[n, pl.ds(NV * v + w, 1), :] * values[w]
                u[v, n, rows, :] = source[v, n, rows, :] - total
            return c

        lax.fori_loop(0, ROWS // CHUNK, one, 0)

    def stores(g, kind):
        buffer, target = ((u, new_ref), (res, res_ref))[kind]
        return [
            pltpu.make_async_copy(buffer.at[v, g, nodes, :], target.at[g, v, :, 0, :], out_s.at[kind, v, g])
            for v in range(NV)
        ]

    def results(g):
        for v in range(NV):
            res[v, g] = metric[...] * r[g, pl.ds(ROWS * v, ROWS), :] + spec[v, g]
        for store in stores(g, 1):
            store.start()

    def weight(offset, n, m):
        return jnp.where(ahead, coupling(4 * offset + n - m), coupling(-4 * offset + n - m)).astype(F32)

    def tiles(body):
        def one(c, carry):
            body(pl.ds(pl.multiple_of(c * 16, 16), 16))
            return carry

        lax.fori_loop(0, 8, one, 0)

    def combine(total, offset, n, values):
        for m in range(4):
            total = total + weight(offset, n, m) * values[m]
        return total

    def own_part(total, n, values):
        for m in range(4):
            if n != m:
                total = total + coupling(n - m) * values[m]
        return total

    def send_cross(g, v):
        def body(rows):
            mine = [us[v, m, rows, :] for m in range(4)]
            theirs = [raw[v, m, rows, :] for m in range(4)]
            for n in (g,):
                for q in range(2):
                    total = combine(jnp.zeros((16, 128), F32), 1 + q, n, mine)
                    cross_out[v, n, q, rows, :] = combine(total, 2 + q, n, theirs)

        tiles(body)
        cross_copy(g, v).start()

    def whole_sums(v):
        near_copy(v).wait_recv()
        far_copy(v).wait_recv()

        def body(rows):
            mine = [us[v, m, rows, :] for m in range(4)]
            theirs = [raw[v, m, rows, :] for m in range(4)]
            near = [near_in[v, m, rows, :] for m in range(4)]
            far = [far_in[v, m, rows, :] for m in range(4)]
            for n in range(4):
                zero = jnp.zeros((16, 128), F32)
                edge_out[v, n, rows, :] = combine(combine(combine(zero, -1, n, mine), -2, n, near), -3, n, far)
                spec[v, n, rows, :] = combine(
                    combine(combine(own_part(zero, n, mine), 1, n, theirs), -1, n, near), -2, n, far
                )

        tiles(body)
        for g in range(2):
            edge_copy(g, v).start()

    def inner_sums(g, v):
        cross_copy(g, v).wait_recv()

        def body(rows):
            mine = [us[v, m, rows, :] for m in range(4)]
            theirs = [raw[v, m, rows, :] for m in range(4)]
            for n in (g,):
                edge_out[v, n, rows, :] = combine(cross_in[v, n, 1, rows, :], -1, n, mine)
                spec[v, n, rows, :] = combine(own_part(cross_in[v, n, 0, rows, :], n, mine), 1, n, theirs)

        tiles(body)
        edge_copy(g, v).start()

    def outer_sums(g, v):
        edge_copy(g, v).wait_recv()

        def body(rows):
            mine = [us[v, m, rows, :] for m in range(4)]
            for n in (g,):
                spec[v, n, rows, :] = own_part(edge_in[v, n, rows, :], n, mine)

        tiles(body)

    def sums(g):
        @pl.when(inner)
        def _():
            for v in range(WHOLE if g >= 2 else NV - 1, NV):
                inner_sums(g, v)

        @pl.when(outer)
        def _():
            for v in range(NV):
                outer_sums(g, v)

    def advance(source, x, g):
        finish(source, g)
        extract(u, x + 1, g)
        send_faces(x + 1, g)

        @pl.when(x == PASSES - 1)
        def _():
            for store in stores(g, 0):
                store.start()

        local_part(u, g)

    each(lambda g: local_part(us, g))
    each(lambda g: pass_on(0, g))

    @pl.when(inner)
    def _():
        for v in range(WHOLE):
            raw_copy(v).wait_recv()
            far_copy(v).start()
        for v in range(WHOLE, NV):
            raw_copy(v).wait_recv()
            for g in range(2):
                send_cross(g, v)
            if v - WHOLE < WHOLE:
                whole_sums(v - WHOLE)
        for g in range(2, INSTANCES):
            for v in range(WHOLE, NV):
                send_cross(g, v)
        for v in range(WHOLE, NV - 1):
            for g in range(2):
                inner_sums(g, v)

    each(lambda g: trace_part(0, g))

    for g in range(INSTANCES):
        sums(g)
        if g == 1:

            @pl.when(inner)
            def _():
                for n in range(2, INSTANCES):
                    for v in range(WHOLE):
                        edge_copy(n, v).start()

        advance(us, 0, g)
        if g > 0:
            pass_on(1, g - 1)
    pass_on(1, INSTANCES - 1)

    def middle(i, c):
        x, g = 1 + i // INSTANCES, lax.rem(i, INSTANCES)
        trace_part(x, g)

        @pl.when(g > 0)
        def _():
            pass_on(x + 1, g - 1)

        advance(u, x, g)

        @pl.when(g == INSTANCES - 1)
        def _():
            pass_on(x + 1, g)

        return c

    lax.fori_loop(0, (PASSES - 1) * INSTANCES, middle, 0)

    def end(g):
        trace_part(PASSES, g)
        results(g)

    each(end)

    def drain(g):
        for kind in range(2):
            for store in stores(g, kind):
                store.wait()
        for x in range(PASSES + 1):
            for f in range(4):
                sending(x, g, f, lambda copy: copy.wait_send())
            for f in range(2):

                @pl.when(route(f, x)[1])
                def _(x=x, f=f):
                    on_copy(x, g, f).wait_send()

    each(drain)

    @pl.when(outer)
    def _():
        for v in range(NV):
            raw_copy(v).wait_send()

    @pl.when(inner)
    def _():
        for v in range(WHOLE):
            near_copy(v).wait_send()
            far_copy(v).wait_send()
        for g in range(INSTANCES):
            for v in range(NV):
                if v >= WHOLE:
                    cross_copy(g, v).wait_send()
                edge_copy(g, v).wait_send()


def per_device(state, metric_scale, flux_jacobians, preconditioner, inflow):
    vmem = pl.BlockSpec(memory_space=pltpu.VMEM)
    smem = pl.BlockSpec(memory_space=pltpu.SMEM)
    block = (4, NV, NODES, 1, 128)
    hbm = pl.BlockSpec(memory_space=pl.ANY)
    dma = pltpu.SemaphoreType.DMA
    exchanges = PASSES + 1
    groups = INSTANCES
    new_state, residual = pl.pallas_call(
        kernel,
        name="pseudo_step",
        out_shape=(pltpu.VMEM(block, F32), pltpu.VMEM(block, F32)),
        in_specs=[hbm, hbm, smem, hbm, vmem, vmem],
        out_specs=(vmem, vmem),
        scratch_shapes=[
            pltpu.VMEM((NV, 4, ROWS, 128), F32),
            pltpu.VMEM((NV, 4, ROWS, 128), F32),
            pltpu.VMEM((NV, 4, ROWS, 128), F32),
            pltpu.VMEM((NV, 4, ROWS, 128), F32),
            pltpu.VMEM((ROWS, 128), F32),
            pltpu.VMEM((4, NV * NV, 128), F32),
            pltpu.VMEM((NV, 4, 32, 128), F32),
            pltpu.VMEM((2 * NV * ROWS, 7 * ROWS), BF16),
            pltpu.VMEM((2 * NV * ROWS, 4 * ROWS), BF16),
            pltpu.VMEM((7 * ROWS, 128), BF16),
            pltpu.VMEM((7 * ROWS, 128), BF16),
            pltpu.VMEM((4 * ROWS, 128), BF16),
            pltpu.VMEM((4 * ROWS, 128), BF16),
            pltpu.VMEM((4, NV * ROWS, 128), F32),
            pltpu.VMEM((2, ROWS, 128), F32),
            pltpu.VMEM((exchanges, 4, 4, ROWS, 128), F32),
            pltpu.VMEM((exchanges, 4, 4, ROWS, 128), F32),
            pltpu.VMEM((exchanges, 4, 4, ROWS, 128), F32),
            pltpu.VMEM((NV, 4, ROWS, 128), F32),
            pltpu.VMEM((WHOLE, 4, ROWS, 128), F32),
            pltpu.VMEM((WHOLE, 4, ROWS, 128), F32),
            pltpu.VMEM((NV, 4, 2, ROWS, 128), F32),
            pltpu.VMEM((NV, 4, 2, ROWS, 128), F32),
            pltpu.VMEM((NV, 4, ROWS, 128), F32),
            pltpu.VMEM((NV, 4, ROWS, 128), F32),
            dma((exchanges, groups, 4)),
            dma((exchanges, groups, 4)),
            dma((exchanges, groups, 4)),
            dma((exchanges, groups, 4)),
            dma((exchanges, groups, 4)),
            dma((NV,)),
            dma((NV,)),
            dma((WHOLE,)),
            dma((WHOLE,)),
            dma((WHOLE,)),
            dma((WHOLE,)),
            dma((groups, NV)),
            dma((groups, NV)),
            dma((groups, NV)),
            dma((groups, NV)),
            dma((NV + 2, 4)),
            dma((2, NV, 4)),
        ],
        compiler_params=pltpu.CompilerParams(
            collective_id=0, has_side_effects=True, vmem_limit_bytes=60 * 2**20
        ),
    )(
        state.reshape(block),
        metric_scale.reshape(NODES, 1, 128),
        flux_jacobians.transpose(1, 0, 2),
        preconditioner.reshape(4, NV * NV, 1, 128),
        inflow.reshape(4, NV, 1, FACE),
        jnp.asarray(patterns()),
    )
    return new_state.reshape(state.shape), residual.reshape(state.shape)


def solution(mesh):
    in_specs = (
        P("tm", None, "elem", None, None),
        P("elem", None, None),
        P(),
        P("tm", None, None, "elem", None),
        P("tm", None, "elem", None),
    )
    out_specs = (P("tm", None, "elem", None, None), P("tm", None, "elem", None, None))
    return jax.shard_map(
        per_device, mesh=mesh, in_specs=in_specs, out_specs=out_specs, check_vma=False
    )
```
